256 devices in a mesh: freq: 8 (over x, z_hi), strip: 32 (over z_lo, y, core).
Axes of the slice: x: 4, y: 4, z: 8 (z_hi: 2, z_lo: 4; z = z_hi * 4 + z_lo), core: 2. Of those that a mesh axis runs over, the one named last changes fastest.
Arguments:
- source_field: float32 [2, 16, 1024, 1024], P(None, 'freq', 'strip'), may hold values from -6 to 6
- receiver_field: float32 [2, 16, 1024, 1024], P(None, 'freq', 'strip'), may hold values from -6 to 6
- velocity: float32 [8, 1024, 1024], P('freq', 'strip'), may hold values from 0.625 to 1.6
- slice_owner: int32 [8], replicated, may hold values from 0 to 7, each once
Outputs:
- depth_image: float32 [2, 1024, 1024], P(None, 'strip', 'freq')
- source_out: float32 [2, 16, 1024, 1024], P(None, 'freq', 'strip')
- receiver_out: float32 [2, 16, 1024, 1024], P(None, 'freq', 'strip')
The draws below stay inside these ranges and needn't reach their ends.
Inputs may be any that keep to these rules, and one draw needn't show every extreme that they name: A permutation of the 8 velocity slices; depth step d reads slice slice_owner[d], which index slice_owner[d] // 1 of freq holds.
All inputs are finite; a program needn't handle non-finite values.
Results may differ from the reference program's by a relative error of at most 0.00011.
Values sent between devices are 32-bit elements; how exact they have to be, the bound alone decides.
A program may use at most 64 MiB of HBM per device.

```python
import math
import jax
import jax.numpy as jnp
from jax import lax

NX = 1024
NY = 1024
DEPTHS = 2
NFREQ = 16
VSLICES = 8


def block_scale(rng, dims, pieces, least, top_value):
    gain = 1.0
    for dim, blocks in pieces:
        heights = jax.random.uniform(jax.random.fold_in(jax.random.fold_in(rng, 6), dim), (blocks,), jnp.float32, least / len(pieces), top_value / len(pieces))
        gain = gain * jnp.repeat(jnp.exp(heights), dims[dim] // blocks).reshape((-1,) + (1,) * (len(dims) - 1 - dim))
    return gain


def noise(own_key, extent, spread, bound, split=(), kind=jnp.bfloat16):
    gain = block_scale(own_key, extent, split, -0.22, 0.18) if split else 1.0
    array = jax.random.normal(own_key, extent, jnp.float32) * spread * gain
    return jnp.minimum(jnp.maximum(array, -bound), bound).astype(kind)


def setup_inputs(seed: int = 0) -> dict:
    seeds = jax.random.split(jax.random.key(seed), 5)
    source_field = noise(seeds[0], (2, NFREQ, NX, NY), 1.0, 6.0, ((1, 8), (2, 32)), jnp.float32)
    receiver_field = noise(seeds[1], (2, NFREQ, NX, NY), 1.0, 6.0, ((1, 8), (2, 32)), jnp.float32)
    velocity = jnp.clip(jnp.exp(math.log(1.6) - 0.94000727 * jax.random.uniform(seeds[2], (VSLICES, NX, NY), jnp.float32) ** block_scale(seeds[2], (VSLICES, NX, NY), ((0, 8), (1, 32)), -0.2, 0.2)), 0.625, 1.6)
    slice_owner = jax.random.permutation(seeds[3], VSLICES).astype(jnp.int32)
    return {"source_field": source_field, "receiver_field": receiver_field, "velocity": velocity, "slice_owner": slice_owner}


step_length = 0.15
omega_top = 1.2
stencil_gain = 0.05
stencil_damping = 0.1

def centered(length):
    position = jnp.arange(length, dtype=jnp.int32)
    shifted = jnp.where(position < length // 2, position, position - length)
    return shifted.astype(jnp.float32) * (2.0 * math.pi / length)

def laplace(field):
    padded = jnp.pad(field, ((0, 0), (1, 1), (1, 1)))
    return padded[:, 2:, 1:-1] + padded[:, :-2, 1:-1] + padded[:, 1:-1, 2:] + padded[:, 1:-1, :-2] - 4.0 * field

def reference(source_field, receiver_field, velocity, slice_owner):
    wave_x = centered(NX)
    wave_y = centered(NY)
    angular = (omega_top * (jnp.arange(NFREQ, dtype=jnp.int32) + 1).astype(jnp.float32) / NFREQ)[:, None, None]
    argument = angular * angular - (wave_x[:, None] * wave_x[:, None] + wave_y[None, :] * wave_y[None, :])[None]
    radius = jnp.sqrt(jnp.abs(argument))
    travel = argument >= 0.0
    trans_real = jnp.where(travel, jnp.cos(step_length * radius), jnp.exp(-step_length * radius))
    trans_imag = jnp.where(travel, jnp.sin(step_length * radius), jnp.zeros_like(radius))
    fields = [lax.complex(source_field[0], source_field[1]), lax.complex(receiver_field[0], receiver_field[1])]
    field_signs = [-1.0, 1.0]
    images = []
    for depth_step in range(DEPTHS):
        speed = lax.dynamic_index_in_dim(velocity, slice_owner[depth_step], 0, keepdims=False)
        gap = 1.0 / speed - 1.0
        weight = stencil_gain * (speed * speed - 1.0)[None] * angular / omega_top
        updated = []
        for which in range(2):
            sign_value = field_signs[which]
            transfer = lax.complex(trans_real, sign_value * trans_imag)
            field = jnp.fft.ifft2(jnp.fft.fft2(fields[which], axes=(1, 2)) * transfer, axes=(1, 2))
            phase = sign_value * angular * step_length * gap[None]
            field = field * lax.complex(jnp.cos(phase), jnp.sin(phase))
            coefficient = lax.complex(stencil_damping * weight, sign_value * weight)
            field = field + coefficient * laplace(field)
            updated.append(field)
        fields = updated
        images.append(lax.optimization_barrier(jnp.sum(jnp.real(fields[0]) * jnp.real(fields[1]) + jnp.imag(fields[0]) * jnp.imag(fields[1]), axis=0)))
    depth_image = jnp.stack(images)
    source_out = jnp.stack([jnp.real(fields[0]), jnp.imag(fields[0])])
    receiver_out = jnp.stack([jnp.real(fields[1]), jnp.imag(fields[1])])
    return (depth_image, source_out, receiver_out)
```

```python
import functools
import math

import jax
import jax.numpy as jnp
import numpy as np
from jax import lax
from jax.experimental import pallas as pl
from jax.experimental.pallas import tpu as pltpu
from jax.sharding import PartitionSpec as P

DEPTHS = 2
N = 1024
Q = 256
step_length = 0.15
omega_top = 1.2
stencil_gain = 0.05
stencil_damping = 0.1
F32 = jnp.float32
BF16 = jnp.bfloat16


def host_tables():
    i = np.arange(Q)
    ang = 2.0 * np.pi * ((i[:, None] * i[None, :]) % Q) / Q
    cs = np.concatenate([np.cos(ang), np.sin(ang)], 0).astype(np.float32)
    hi = cs.astype(jnp.bfloat16)
    lo = (cs - hi.astype(np.float32)).astype(jnp.bfloat16)
    k = np.arange(4)
    tang = 2.0 * np.pi * (k[:, None] * i[None, :]) / N
    twy = np.concatenate([np.cos(tang), np.sin(tang)], 0).astype(np.float32)
    return hi, lo, twy


def split(x):
    hi = x.astype(BF16)
    lo = (x - hi.astype(F32)).astype(BF16)
    return hi, lo


def mm(a, b):
    return jnp.dot(a, b, preferred_element_type=F32)


def radix4(x, sign):
    (ar, ai), (br, bi), (cr, ci), (dr, di) = x
    t0r, t0i, t1r, t1i = ar + cr, ai + ci, ar - cr, ai - ci
    t2r, t2i, t3r, t3i = br + dr, bi + di, br - dr, bi - di
    o0 = (t0r + t2r, t0i + t2i)
    o2 = (t0r - t2r, t0i - t2i)
    minus = (t1r + t3i, t1i - t3r)
    plus = (t1r - t3i, t1i + t3r)
    return (o0, minus, o2, plus) if sign < 0 else (o0, plus, o2, minus)


def forward_y(xr, xi, fh, fl, twy):
    rows = xr.shape[0]
    parts = [(xr[:, Q * n : Q * n + Q], xi[:, Q * n : Q * n + Q]) for n in range(4)]
    b = radix4(parts, -1)
    stack = []
    for k in range(4):
        r, m = b[k]
        if k:
            c, s = twy[k : k + 1, :], twy[4 + k : 5 + k, :]
            r, m = r * c + m * s, m * c - r * s
        stack += [r, m]
    hi, lo = split(jnp.concatenate(stack, 0))
    pc = mm(hi, fh[:Q]) + mm(lo, fh[:Q]) + mm(hi, fl[:Q])
    ps = mm(hi, fh[Q:]) + mm(lo, fh[Q:]) + mm(hi, fl[Q:])
    out = []
    for k in range(4):
        a, z, e = 2 * k * rows, (2 * k + 1) * rows, (2 * k + 2) * rows
        out.append((pc[a:z] + ps[z:e], pc[z:e] - ps[a:z]))
    return out


def phase_a(src_ref, rcv_ref, send_ref, fh_ref, fl_ref, twy_ref):
    fh, fl, twy = fh_ref, fl_ref, twy_ref[...]
    for f in range(2):
        for p, ref in enumerate((src_ref, rcv_ref)):
            xr, xi = ref[0, f], ref[1, f]
            if p:
                xi = -xi
            out = forward_y(xr, xi, fh[...], fl[...], twy)
            for k in range(4):
                for half in range(2):
                    d = f * 16 + p * 8 + 2 * k + half
                    send_ref[d, 0:32, :] = out[k][0][:, 128 * half : 128 * half + 128]
                    send_ref[d, 32:64, :] = out[k][1][:, 128 * half : 128 * half + 128]


def phase_b(load, store, h_ref, fh_ref, fl_ref, twx_ref, bh_ref, bl_ref, g_ref):
    for s8 in range(8):
        x = radix4([load(n1, s8) for n1 in range(4)], -1)
        sl = slice(32 * s8, 32 * s8 + 32)
        for k in range(4):
            r, m = x[k]
            if k:
                c, s = twx_ref[k - 1, sl, :], twx_ref[2 + k, sl, :]
                r, m = r * c + m * s, m * c - r * s
            rh, rl = split(r)
            mh, ml = split(m)
            bh_ref[k, sl, 0:128] = rh
            bl_ref[k, sl, 0:128] = rl
            bh_ref[k, sl, 128:256] = mh
            bl_ref[k, sl, 128:256] = ml
    for k in range(4):
        fh, fl = fh_ref[...], fl_ref[...]
        bh = bh_ref[k]
        pr = mm(fh, bh) + mm(fl, bh) + mm(fh, bl_ref[k])
        re = pr[:Q, :128] + pr[Q:, 128:]
        im = pr[:Q, 128:] - pr[Q:, :128]
        hr, hi_ = h_ref[k], h_ref[4 + k]
        zr = re * hr - im * hi_
        zi = re * hi_ + im * hr
        zh, zl = split(jnp.concatenate([zr, zi], 1))
        pr = mm(fh, zh) + mm(fl, zh) + mm(fh, zl)
        re = pr[:Q, :128] - pr[Q:, 128:]
        im = pr[:Q, 128:] + pr[Q:, :128]
        if k:
            c, s = twx_ref[k - 1], twx_ref[2 + k]
            re, im = re * c - im * s, im * c + re * s
        g_ref[k, :, 0:128] = re
        g_ref[k, :, 128:256] = im
    for s8 in range(8):
        sl = slice(32 * s8, 32 * s8 + 32)
        x = radix4([(g_ref[k, sl, 0:128], g_ref[k, sl, 128:256]) for k in range(4)], 1)
        for n1 in range(4):
            store(8 * n1 + s8, *x[n1])


def store_16(send_ref):
    zero = jnp.zeros((1, 128), F32)

    def store(s, re, im):
        d, t = s % 16, s // 16
        send_ref[d, 64 * t : 64 * t + 32, :] = re
        send_ref[d, 64 * t + 32 : 64 * t + 64, :] = im
        if s < 31:
            d, t = (s + 1) % 16, (s + 1) // 16
            send_ref[d, 128 + 2 * t : 129 + 2 * t, :] = re[31:32]
            send_ref[d, 132 + 2 * t : 133 + 2 * t, :] = im[31:32]
        else:
            send_ref[15, 131:132, :] = zero
            send_ref[15, 135:136, :] = zero
        if s > 0:
            d, t = (s - 1) % 16, (s - 1) // 16
            send_ref[d, 129 + 2 * t : 130 + 2 * t, :] = re[0:1]
            send_ref[d, 133 + 2 * t : 134 + 2 * t, :] = im[0:1]
        else:
            send_ref[0, 128:129, :] = zero
            send_ref[0, 132:133, :] = zero

    return store


def store_32(send_ref):
    zero = jnp.zeros((1, 128), F32)

    def store(s, re, im):
        send_ref[s, 0:32, :] = re
        send_ref[s, 32:64, :] = im
        if s < 31:
            send_ref[s + 1, 64:65, :] = re[31:32]
            send_ref[s + 1, 66:67, :] = im[31:32]
        else:
            send_ref[31, 65:66, :] = zero
            send_ref[31, 67:68, :] = zero
        send_ref[s, 68:72, :] = jnp.zeros((4, 128), F32)
        if s > 0:
            send_ref[s - 1, 65:66, :] = re[0:1]
            send_ref[s - 1, 67:68, :] = im[0:1]
        else:
            send_ref[0, 64:65, :] = zero
            send_ref[0, 66:67, :] = zero

    return store


def inverse_y(blocks, pairs, fh_ref, fl_ref, twy, pc_ref, ps_ref, g_ref):
    for k in range(4):
        x = jnp.concatenate([blocks(k, 0), blocks(k, 1)], 1)
        hi, lo = split(x)
        pc_ref[...] = mm(hi, fh_ref[:Q]) + mm(lo, fh_ref[:Q]) + mm(hi, fl_ref[:Q])
        ps_ref[...] = mm(hi, fh_ref[Q:]) + mm(lo, fh_ref[Q:]) + mm(hi, fl_ref[Q:])
        for a, b, n in pairs:
            re = pc_ref[a : a + n] - ps_ref[b : b + n]
            im = pc_ref[b : b + n] + ps_ref[a : a + n]
            if k:
                c, s = twy[k : k + 1, :], twy[4 + k : 5 + k, :]
                re, im = re * c - im * s, im * c + re * s
            g_ref[k, a : a + n, :] = re
            g_ref[k, b : b + n, :] = im


def corrected(g_ref, a, b, n, rot):
    x = radix4([(g_ref[k, a : a + n, :], g_ref[k, b : b + n, :]) for k in range(4)], 1)
    re = jnp.concatenate([x[i][0] for i in range(4)], 1)
    im = jnp.concatenate([x[i][1] for i in range(4)], 1)
    c, s = rot
    return re * c + im * s, im * c - re * s


def rotation(speed, angular):
    ph = angular * step_length * (1.0 / speed - 1.0)
    u = ph * ph
    c = 1.0 + u * (-0.5 + u * (1.0 / 24 + u * (-1.0 / 720)))
    s = ph * (1.0 + u * (-1.0 / 6 + u * (1.0 / 120 + u * (-1.0 / 5040))))
    return c, s


def laplace(ref, idx, lane):
    mid = ref[idx, 8:40, :]
    left = jnp.where(lane == 0, 0.0, pltpu.roll(mid, 1, 1))
    right = jnp.where(lane == N - 1, 0.0, pltpu.roll(mid, N - 1, 1))
    beside = ref[idx, 9:41, :] + ref[idx, 7:39, :]
    return mid, beside + left + right - 4.0 * mid


def continued(fld_ref, i, weight, lane):
    pr, lr = laplace(fld_ref, 2 * i, lane)
    pi_, li = laplace(fld_ref, 2 * i + 1, lane)
    return (
        pr + weight * (stencil_damping * lr + li),
        pi_ + weight * (stencil_damping * li - lr),
    )


def weight_of(speed, angular):
    return stencil_gain * (speed * speed - 1.0) * angular / omega_top


def phase_c(recv_ref, vel_ref, vhalo_ref, angular, send_ref, img_ref, scr, tabs):
    fh_ref, fl_ref, twy_ref = tabs
    pc_ref, ps_ref, g_ref, fld_ref, tmp_ref = scr
    twy = twy_ref[...]
    pairs = []
    for p in range(2):
        o = 136 * p
        pairs += [(o, o + 32, 32), (o + 64, o + 96, 32), (o + 128, o + 132, 4)]

    def blocks(k, half):
        return jnp.concatenate([recv_ref[2 * k + half], recv_ref[8 + 2 * k + half]], 0)

    inverse_y(blocks, pairs, fh_ref, fl_ref, twy, pc_ref, ps_ref, g_ref)
    lane = lax.broadcasted_iota(jnp.int32, (32, N), 1)
    hrot = rotation(vhalo_ref[0:4, :], angular)
    for p in range(2):
        o = 136 * p + 128
        re, im = corrected(g_ref, o, o + 4, 4, hrot)
        tmp_ref[4 * p : 4 * p + 4, :] = re
        tmp_ref[8 + 4 * p : 12 + 4 * p, :] = im
    for t in range(2):
        speed = vel_ref[t]
        rot = rotation(speed, angular)
        weight = weight_of(speed, angular)
        outs = []
        for p in range(2):
            o = 136 * p + 64 * t
            re, im = corrected(g_ref, o, o + 32, 32, rot)
            fld_ref[2 * p, 8:40, :] = re
            fld_ref[2 * p + 1, 8:40, :] = im
            for c in range(2):
                r = 8 * c + 4 * p + 2 * t
                fld_ref[2 * p + c, 7:8, :] = tmp_ref[r : r + 1, :]
                fld_ref[2 * p + c, 40:41, :] = tmp_ref[r + 1 : r + 2, :]
            re, im = continued(fld_ref, p, weight, lane)
            outs.append((re, im))
            out = forward_y(re, im, fh_ref[...], fl_ref[...], twy)
            for k in range(4):
                for half in range(2):
                    d = p * 8 + 2 * k + half
                    ls = slice(128 * half, 128 * half + 128)
                    send_ref[d, 64 * t : 64 * t + 32, :] = out[k][0][:, ls]
                    send_ref[d, 64 * t + 32 : 64 * t + 64, :] = out[k][1][:, ls]
        img_ref[t] = outs[0][0] * outs[1][0] - outs[0][1] * outs[1][1]


def phase_e(recv_ref, vel_ref, vhalo_ref, angulars, src_ref, rcv_ref, img_ref, scr, tabs):
    fh_ref, fl_ref, twy_ref = tabs
    pc_ref, ps_ref, g_ref, fld_ref, tmp_ref = scr
    twy = twy_ref[...]
    pairs = []
    for i in range(4):
        o = 72 * i
        pairs += [(o, o + 32, 32), (o + 64, o + 66, 2)]

    def blocks(k, half):
        return jnp.concatenate([recv_ref[8 * i + 2 * k + half] for i in range(4)], 0)

    inverse_y(blocks, pairs, fh_ref, fl_ref, twy, pc_ref, ps_ref, g_ref)
    lane = lax.broadcasted_iota(jnp.int32, (32, N), 1)
    speed = vel_ref[...]
    for f in range(2):
        rot = rotation(speed, angulars[f])
        hrot = rotation(vhalo_ref[0:2, :], angulars[f])
        weight = weight_of(speed, angulars[f])
        outs = []
        for p in range(2):
            o = 72 * (2 * f + p)
            re, im = corrected(g_ref, o + 64, o + 66, 2, hrot)
            tmp_ref[0:2, :] = re
            tmp_ref[8:10, :] = im
            re, im = corrected(g_ref, o, o + 32, 32, rot)
            fld_ref[2 * p, 8:40, :] = re
            fld_ref[2 * p + 1, 8:40, :] = im
            for c in range(2):
                fld_ref[2 * p + c, 7:8, :] = tmp_ref[8 * c : 8 * c + 1, :]
                fld_ref[2 * p + c, 40:41, :] = tmp_ref[8 * c + 1 : 8 * c + 2, :]
            re, im = continued(fld_ref, p, weight, lane)
            outs.append((re, im))
            ref = (src_ref, rcv_ref)[p]
            ref[0, f] = re
            ref[1, f] = -im if p else im
        term = outs[0][0] * outs[1][0] - outs[0][1] * outs[1][1]
        img_ref[...] = img_ref[...] + term if f else term


def centered(position):
    shifted = jnp.where(position < N // 2, position, position - N)
    return shifted.astype(F32) * (2.0 * math.pi / N)


def transfer_table(angular, yc):
    k1 = jnp.arange(4, dtype=jnp.int32)[:, None, None]
    k2 = jnp.arange(Q, dtype=jnp.int32)[None, :, None]
    lane = jnp.arange(128, dtype=jnp.int32)[None, None, :]
    wx = centered(4 * k2 + k1)
    wy = centered(4 * ((yc % 2) * 128 + lane) + yc // 2)
    a = angular * angular - (wx * wx + wy * wy)
    r = jnp.sqrt(jnp.abs(a))
    travel = a >= 0.0
    scale = 1.0 / (N * N)
    re = jnp.where(travel, jnp.cos(step_length * r), jnp.exp(-step_length * r)) * scale
    im = jnp.where(travel, -jnp.sin(step_length * r), 0.0) * scale
    return jnp.concatenate([re, im], 0)


VM = pl.BlockSpec(memory_space=pltpu.VMEM)
SM = pl.BlockSpec(memory_space=pltpu.SMEM)
PARAMS = pltpu.CompilerParams(vmem_limit_bytes=48 << 20)


def call(fn, outs, ins, scratch, n_smem=0, name=None):
    return pl.pallas_call(
        fn,
        out_shape=[jax.ShapeDtypeStruct(o, F32) for o in outs],
        in_specs=[SM] * n_smem + [VM] * (len(ins) - n_smem),
        out_specs=[VM] * len(outs),
        scratch_shapes=scratch,
        compiler_params=PARAMS,
        name=name,
    )(*ins)


def scratch_y(rows):
    return [
        pltpu.VMEM((rows, Q), F32),
        pltpu.VMEM((rows, Q), F32),
        pltpu.VMEM((4, rows, Q), F32),
        pltpu.VMEM((4, 48, N), F32),
        pltpu.VMEM((16, N), F32),
    ]


SCR_B = [
    pltpu.VMEM((4, Q, Q), BF16),
    pltpu.VMEM((4, Q, Q), BF16),
    pltpu.VMEM((4, Q, Q), F32),
]
G16 = [[16 * h + i for i in range(16)] for h in range(2)]


def local(source_field, receiver_field, velocity, slice_owner):
    hi, lo, twy_np = host_tables()
    fh, fl, twy = jnp.asarray(hi), jnp.asarray(lo), jnp.asarray(twy_np)
    twx = jnp.broadcast_to(
        jnp.asarray(np.concatenate([twy_np[1:4], twy_np[5:8]], 0))[:, :, None], (6, Q, 128)
    )
    freq, strip = lax.axis_index("freq"), lax.axis_index("strip")
    h, yc = strip // 16, strip % 8
    ang = [omega_top * (2 * freq + f + 1).astype(F32) / 16 for f in range(2)]
    ang_h = jnp.where(h == 0, ang[0], ang[1])
    table = transfer_table(ang_h, yc)

    slices = [velocity[0]] + [
        lax.ppermute(velocity[0], "freq", [(i, (i + 2 * k) % 8) for i in range(8)])
        for k in range(1, 4)
    ]
    mine = []
    for d in range(DEPTHS):
        acc = jnp.zeros_like(slices[0])
        for k in range(4):
            acc = acc + jnp.where(slice_owner[d] == (freq - 2 * k) % 8, slices[k], 0.0)
        mine.append(acc)
    mine = jnp.stack(mine)
    speed = mine + lax.ppermute(mine, "freq", [(i, i ^ 1) for i in range(8)])
    top = lax.ppermute(speed[:, 31:32], "strip", [(i, i + 1) for i in range(31)])
    bot = lax.ppermute(speed[:, 0:1], "strip", [(i + 1, i) for i in range(31)])
    halo = jnp.concatenate([top, bot], 1)
    halo = jnp.where(halo == 0.0, 1.0, halo)
    own0 = jnp.concatenate([speed[0], halo[0], jnp.ones((6, N), F32)], 0)
    par0 = lax.ppermute(own0, "strip", [(i, i ^ 16) for i in range(32)])
    first = jnp.where(h == 0, own0, par0)
    second = jnp.where(h == 0, par0, own0)
    vel0 = jnp.stack([first[:32], second[:32]])
    vhalo0 = jnp.concatenate([first[32:34], second[32:34], jnp.ones((4, N), F32)], 0)
    vhalo1 = jnp.concatenate([halo[1], jnp.ones((6, N), F32)], 0)

    tabs = (fh, fl, twy)

    def k_a(s, r, a, b, c, o):
        phase_a(s, r, o, a, b, c)

    (send1,) = call(k_a, [(32, 64, 128)], (source_field, receiver_field, *tabs), [], name="phase_a")
    recv1 = lax.all_to_all(send1, "strip", 0, 0, tiled=True)

    def k_b(x, hh, a, b, t, o, bh, bl, g):
        phase_b(
            lambda n1, s8: (x[8 * n1 + s8, 0:32, :], x[8 * n1 + s8, 32:64, :]),
            store_16(o), hh, a, b, t, bh, bl, g,
        )

    (send2,) = call(k_b, [(16, 136, 128)], (recv1, table, fh, fl, twx), SCR_B, name="phase_b")
    recv2 = lax.all_to_all(send2, "strip", 0, 0, tiled=True, axis_index_groups=G16)

    def k_c(a_s, x, v, vh, a, b, c, o, im, *scr):
        phase_c(x, v, vh, a_s[0], o, im, scr, (a, b, c))

    send3, img0 = call(
        k_c, [(16, 128, 128), (2, 32, N)], (ang_h[None], recv2, vel0, vhalo0, *tabs),
        scratch_y(272), n_smem=1, name="phase_c",
    )
    recv3 = lax.all_to_all(send3, "strip", 0, 0, tiled=True, axis_index_groups=G16)

    def k_d(x, hh, a, b, t, o, bh, bl, g):
        def load(n1, s8):
            i, o = 8 * (n1 % 2) + s8, 64 * (n1 // 2)
            return x[i, o : o + 32, :], x[i, o + 32 : o + 64, :]

        phase_b(load, store_32(o), hh, a, b, t, bh, bl, g)

    (send4,) = call(k_d, [(32, 72, 128)], (recv3, table, fh, fl, twx), SCR_B, name="phase_d")
    recv4 = lax.all_to_all(send4, "strip", 0, 0, tiled=True)

    def k_e(a_s, x, v, vh, a, b, c, so, ro, im, *scr):
        phase_e(x, v, vh, (a_s[0], a_s[1]), so, ro, im, scr, (a, b, c))

    so, ro, img1 = call(
        k_e, [(2, 2, 32, N), (2, 2, 32, N), (32, N)],
        (jnp.stack(ang), recv4, speed[1], vhalo1, *tabs),
        scratch_y(288), n_smem=1, name="phase_e",
    )
    keep = jnp.where(h == 0, img0[0], img0[1])
    give = jnp.where(h == 0, img0[1], img0[0])
    img0 = keep + lax.ppermute(give, "strip", [(i, i ^ 16) for i in range(32)])
    img = jnp.stack([img0, img1]).reshape(2, 32, 8, 128).transpose(2, 0, 1, 3)
    img = lax.all_to_all(img, "freq", 0, 0, tiled=True)
    return jnp.sum(img, 0), so, ro


def solution(mesh):
    return jax.shard_map(
        local,
        mesh=mesh,
        in_specs=(
            P(None, "freq", "strip", None),
            P(None, "freq", "strip", None),
            P("freq", "strip", None),
            P(),
        ),
        out_specs=(
            P(None, "strip", "freq"),
            P(None, "freq", "strip", None),
            P(None, "freq", "strip", None),
        ),
        check_vma=False,
    )
```

```python
import functools
import math

import jax
import jax.numpy as jnp
import numpy as np
from jax import lax
from jax.experimental import pallas as pl
from jax.experimental.pallas import tpu as pltpu
from jax.sharding import PartitionSpec as P

DEPTHS = 2
N = 1024
Q = 256
step_length = 0.15
omega_top = 1.2
stencil_gain = 0.05
stencil_damping = 0.1
F32 = jnp.float32
BF16 = jnp.bfloat16


def host_tables():
    i = np.arange(Q)
    ang = 2.0 * np.pi * ((i[:, None] * i[None, :]) % Q) / Q
    cs = np.concatenate([np.cos(ang), np.sin(ang)], 0).astype(np.float32)
    hi = cs.astype(jnp.bfloat16)
    lo = (cs - hi.astype(np.float32)).astype(jnp.bfloat16)
    k = np.arange(4)
    tang = 2.0 * np.pi * (k[:, None] * i[None, :]) / N
    twy = np.concatenate([np.cos(tang), np.sin(tang)], 0).astype(np.float32)
    return hi, lo, twy


def split(x):
    hi = x.astype(BF16)
    lo = (x - hi.astype(F32)).astype(BF16)
    return hi, lo


def mm(a, b):
    return jnp.dot(a, b, preferred_element_type=F32)


def radix4(x, sign):
    (ar, ai), (br, bi), (cr, ci), (dr, di) = x
    t0r, t0i, t1r, t1i = ar + cr, ai + ci, ar - cr, ai - ci
    t2r, t2i, t3r, t3i = br + dr, bi + di, br - dr, bi - di
    o0 = (t0r + t2r, t0i + t2i)
    o2 = (t0r - t2r, t0i - t2i)
    minus = (t1r + t3i, t1i - t3r)
    plus = (t1r - t3i, t1i + t3r)
    return (o0, minus, o2, plus) if sign < 0 else (o0, plus, o2, minus)


def forward_y(xr, xi, fh, fl, twy):
    rows = xr.shape[0]
    parts = [(xr[:, Q * n : Q * n + Q], xi[:, Q * n : Q * n + Q]) for n in range(4)]
    b = radix4(parts, -1)
    stack = []
    for k in range(4):
        r, m = b[k]
        if k:
            c, s = twy[k : k + 1, :], twy[4 + k : 5 + k, :]
            r, m = r * c + m * s, m * c - r * s
        stack += [r, m]
    hi, lo = split(jnp.concatenate(stack, 0))
    pc = mm(hi, fh[:Q]) + mm(lo, fh[:Q]) + mm(hi, fl[:Q])
    ps = mm(hi, fh[Q:]) + mm(lo, fh[Q:]) + mm(hi, fl[Q:])
    out = []
    for k in range(4):
        a, z, e = 2 * k * rows, (2 * k + 1) * rows, (2 * k + 2) * rows
        out.append((pc[a:z] + ps[z:e], pc[z:e] - ps[a:z]))
    return out


def phase_a(src_ref, rcv_ref, send_ref, combo, fh_ref, fl_ref, twy):
    f, p = combo // 2, combo % 2
    first = p == 0
    xr = jnp.where(first, src_ref[0, f], rcv_ref[0, f])
    xi = jnp.where(first, src_ref[1, f], -rcv_ref[1, f])
    out = forward_y(xr, xi, fh_ref[...], fl_ref[...], twy)
    for k in range(4):
        for half in range(2):
            d = combo * 8 + 2 * k + half
            send_ref[d, 0:32, :] = out[k][0][:, 128 * half : 128 * half + 128]
            send_ref[d, 32:64, :] = out[k][1][:, 128 * half : 128 * half + 128]


def phase_b(ready, load, store, h_ref, fh_ref, fl_ref, twx_ref, bh_ref, bl_ref, g_ref):
    for s8 in range(8):
        ready(s8)
        x = radix4([load(n1, s8) for n1 in range(4)], -1)
        sl = slice(32 * s8, 32 * s8 + 32)
        for k in range(4):
            r, m = x[k]
            if k:
                c, s = twx_ref[k - 1, sl, :], twx_ref[2 + k, sl, :]
                r, m = r * c + m * s, m * c - r * s
            rh, rl = split(r)
            mh, ml = split(m)
            bh_ref[k, sl, 0:128] = rh
            bl_ref[k, sl, 0:128] = rl
            bh_ref[k, sl, 128:256] = mh
            bl_ref[k, sl, 128:256] = ml
    for k in range(4):
        fh, fl = fh_ref[...], fl_ref[...]
        bh = bh_ref[k]
        pr = mm(fh, bh) + mm(fl, bh) + mm(fh, bl_ref[k])
        re = pr[:Q, :128] + pr[Q:, 128:]
        im = pr[:Q, 128:] - pr[Q:, :128]
        hr, hi_ = h_ref[k], h_ref[4 + k]
        zr = re * hr - im * hi_
        zi = re * hi_ + im * hr
        zh, zl = split(jnp.concatenate([zr, zi], 1))
        pr = mm(fh, zh) + mm(fl, zh) + mm(fh, zl)
        re = pr[:Q, :128] - pr[Q:, 128:]
        im = pr[:Q, 128:] + pr[Q:, :128]
        if k:
            c, s = twx_ref[k - 1], twx_ref[2 + k]
            re, im = re * c - im * s, im * c + re * s
        g_ref[k, :, 0:128] = re
        g_ref[k, :, 128:256] = im
    for s8 in range(8):
        sl = slice(32 * s8, 32 * s8 + 32)
        x = radix4([(g_ref[k, sl, 0:128], g_ref[k, sl, 128:256]) for k in range(4)], 1)
        for n1 in range(4):
            store(8 * n1 + s8, *x[n1])


def store_16(send_ref):
    zero = jnp.zeros((1, 128), F32)

    def store(s, re, im):
        d, t = s % 16, s // 16
        send_ref[d, 64 * t : 64 * t + 32, :] = re
        send_ref[d, 64 * t + 32 : 64 * t + 64, :] = im
        if s < 31:
            d, t = (s + 1) % 16, (s + 1) // 16
            send_ref[d, 128 + 2 * t : 129 + 2 * t, :] = re[31:32]
            send_ref[d, 132 + 2 * t : 133 + 2 * t, :] = im[31:32]
        else:
            send_ref[15, 131:132, :] = zero
            send_ref[15, 135:136, :] = zero
        if s > 0:
            d, t = (s - 1) % 16, (s - 1) // 16
            send_ref[d, 129 + 2 * t : 130 + 2 * t, :] = re[0:1]
            send_ref[d, 133 + 2 * t : 134 + 2 * t, :] = im[0:1]
        else:
            send_ref[0, 128:129, :] = zero
            send_ref[0, 132:133, :] = zero

    return store


def store_32(send_ref):
    zero = jnp.zeros((1, 128), F32)

    def store(s, re, im):
        send_ref[s, 0:32, :] = re
        send_ref[s, 32:64, :] = im
        if s < 31:
            send_ref[s + 1, 64:65, :] = re[31:32]
            send_ref[s + 1, 66:67, :] = im[31:32]
        else:
            send_ref[31, 65:66, :] = zero
            send_ref[31, 67:68, :] = zero
        send_ref[s, 68:72, :] = jnp.zeros((4, 128), F32)
        if s > 0:
            send_ref[s - 1, 65:66, :] = re[0:1]
            send_ref[s - 1, 67:68, :] = im[0:1]
        else:
            send_ref[0, 64:65, :] = zero
            send_ref[0, 66:67, :] = zero

    return store


def inverse_y(ready, blocks, pairs, fh_ref, fl_ref, twy, pc_ref, ps_ref, g_ref):
    for k in range(4):
        ready(k)
        x = jnp.concatenate([blocks(k, 0), blocks(k, 1)], 1)
        hi, lo = split(x)
        pc_ref[...] = mm(hi, fh_ref[:Q]) + mm(lo, fh_ref[:Q]) + mm(hi, fl_ref[:Q])
        ps_ref[...] = mm(hi, fh_ref[Q:]) + mm(lo, fh_ref[Q:]) + mm(hi, fl_ref[Q:])
        for a, b, n in pairs:
            re = pc_ref[a : a + n] - ps_ref[b : b + n]
            im = pc_ref[b : b + n] + ps_ref[a : a + n]
            if k:
                c, s = twy[k : k + 1, :], twy[4 + k : 5 + k, :]
                re, im = re * c - im * s, im * c + re * s
            g_ref[k, a : a + n, :] = re
            g_ref[k, b : b + n, :] = im


def corrected(g_ref, a, b, n, rot):
    x = radix4([(g_ref[k, a : a + n, :], g_ref[k, b : b + n, :]) for k in range(4)], 1)
    re = jnp.concatenate([x[i][0] for i in range(4)], 1)
    im = jnp.concatenate([x[i][1] for i in range(4)], 1)
    c, s = rot
    return re * c + im * s, im * c - re * s


def rotation(speed, angular):
    ph = angular * step_length * (1.0 / speed - 1.0)
    u = ph * ph
    c = 1.0 + u * (-0.5 + u * (1.0 / 24 + u * (-1.0 / 720)))
    s = ph * (1.0 + u * (-1.0 / 6 + u * (1.0 / 120 + u * (-1.0 / 5040))))
    return c, s


def laplace(ref, idx, lane):
    mid = ref[idx, 8:40, :]
    left = jnp.where(lane == 0, 0.0, pltpu.roll(mid, 1, 1))
    right = jnp.where(lane == N - 1, 0.0, pltpu.roll(mid, N - 1, 1))
    beside = ref[idx, 9:41, :] + ref[idx, 7:39, :]
    return mid, beside + left + right - 4.0 * mid


def continued(fld_ref, i, weight, lane):
    pr, lr = laplace(fld_ref, 2 * i, lane)
    pi_, li = laplace(fld_ref, 2 * i + 1, lane)
    return (
        pr + weight * (stencil_damping * lr + li),
        pi_ + weight * (stencil_damping * li - lr),
    )


def weight_of(speed, angular):
    return stencil_gain * (speed * speed - 1.0) * angular / omega_top


def phase_c(ready, sent, recv_ref, vel_ref, htop_ref, hbot_ref, h, angular, send_ref, img_ref, scr, tabs):
    fh_ref, fl_ref, twy_ref = tabs
    pc_ref, ps_ref, g_ref, fld_ref, tmp_ref, hv_ref = scr
    twy = twy_ref[...]
    pairs = []
    for p in range(2):
        o = 136 * p
        pairs += [(o, o + 32, 32), (o + 64, o + 96, 32), (o + 128, o + 132, 4)]

    def blocks(k, half):
        return jnp.concatenate([recv_ref[2 * k + half], recv_ref[8 + 2 * k + half]], 0)

    inverse_y(ready, blocks, pairs, fh_ref, fl_ref, twy, pc_ref, ps_ref, g_ref)
    lane = lax.broadcasted_iota(jnp.int32, (32, N), 1)
    for t in range(2):
        own = h == t
        hv_ref[2 * t : 2 * t + 1, :] = jnp.where(own, htop_ref[0, 0:1, :], htop_ref[1, 0:1, :])
        hv_ref[2 * t + 1 : 2 * t + 2, :] = jnp.where(own, hbot_ref[0, 0:1, :], hbot_ref[1, 0:1, :])
    hrot = rotation(hv_ref[0:4, :], angular)
    for p in range(2):
        o = 136 * p + 128
        re, im = corrected(g_ref, o, o + 4, 4, hrot)
        tmp_ref[4 * p : 4 * p + 4, :] = re
        tmp_ref[8 + 4 * p : 12 + 4 * p, :] = im
    for t in range(2):
        speed = jnp.where(h == t, vel_ref[0], vel_ref[2])
        rot = rotation(speed, angular)
        weight = weight_of(speed, angular)
        outs = []
        for p in range(2):
            o = 136 * p + 64 * t
            re, im = corrected(g_ref, o, o + 32, 32, rot)
            fld_ref[2 * p, 8:40, :] = re
            fld_ref[2 * p + 1, 8:40, :] = im
            for c in range(2):
                r = 8 * c + 4 * p + 2 * t
                fld_ref[2 * p + c, 7:8, :] = tmp_ref[r : r + 1, :]
                fld_ref[2 * p + c, 40:41, :] = tmp_ref[r + 1 : r + 2, :]
            re, im = continued(fld_ref, p, weight, lane)
            outs.append((re, im))
            out = forward_y(re, im, fh_ref[...], fl_ref[...], twy)
            for k in range(4):
                for half in range(2):
                    d = p * 8 + 2 * k + half
                    ls = slice(128 * half, 128 * half + 128)
                    send_ref[t, d, 0:32, :] = out[k][0][:, ls]
                    send_ref[t, d, 32:64, :] = out[k][1][:, ls]
        sent(t)
        img_ref[t] = outs[0][0] * outs[1][0] - outs[0][1] * outs[1][1]


def phase_e(ready, done, recv_ref, speed, htop_ref, hbot_ref, angulars, src_ref, rcv_ref, img_ref, scr, tabs):
    fh_ref, fl_ref, twy_ref = tabs
    pc_ref, ps_ref, g_ref, fld_ref, tmp_ref, hv_ref = scr
    twy = twy_ref[...]
    pairs = []
    for i in range(4):
        o = 72 * i
        pairs += [(o, o + 32, 32), (o + 64, o + 66, 2)]

    def blocks(k, half):
        return jnp.concatenate([recv_ref[8 * i + 2 * k + half] for i in range(4)], 0)

    inverse_y(ready, blocks, pairs, fh_ref, fl_ref, twy, pc_ref, ps_ref, g_ref)
    lane = lax.broadcasted_iota(jnp.int32, (32, N), 1)
    hv_ref[0:1, :] = htop_ref[0, 1:2, :]
    hv_ref[1:2, :] = hbot_ref[0, 1:2, :]
    for f in range(2):
        rot = rotation(speed, angulars[f])
        hrot = rotation(hv_ref[0:2, :], angulars[f])
        weight = weight_of(speed, angulars[f])
        outs = []
        for p in range(2):
            o = 72 * (2 * f + p)
            re, im = corrected(g_ref, o + 64, o + 66, 2, hrot)
            tmp_ref[0:2, :] = re
            tmp_ref[8:10, :] = im
            re, im = corrected(g_ref, o, o + 32, 32, rot)
            fld_ref[2 * p, 8:40, :] = re
            fld_ref[2 * p + 1, 8:40, :] = im
            for c in range(2):
                fld_ref[2 * p + c, 7:8, :] = tmp_ref[8 * c : 8 * c + 1, :]
                fld_ref[2 * p + c, 40:41, :] = tmp_ref[8 * c + 1 : 8 * c + 2, :]
            re, im = continued(fld_ref, p, weight, lane)
            outs.append((re, im))
            ref = (src_ref, rcv_ref)[p]
            ref[0, f] = re
            ref[1, f] = -im if p else im
        term = outs[0][0] * outs[1][0] - outs[0][1] * outs[1][1]
        img_ref[...] = img_ref[...] + term if f else term
        done(f)


def centered(position):
    shifted = jnp.where(position < N // 2, position, position - N)
    return shifted.astype(F32) * (2.0 * math.pi / N)


def transfer_rows(h_ref, k1, angular, yc):
    k2 = lax.broadcasted_iota(jnp.int32, (Q, 128), 0)
    lane = lax.broadcasted_iota(jnp.int32, (Q, 128), 1)
    wx = centered(4 * k2 + k1)
    wy = centered(4 * ((yc % 2) * 128 + lane) + yc // 2)
    a = angular * angular - (wx * wx + wy * wy)
    z = step_length * jnp.sqrt(jnp.abs(a))
    u = z * z
    cos = 1.0 + u * (-0.5 + u * (1.0 / 24 + u * (-1.0 / 720 + u * (1.0 / 40320))))
    sin = z * (1.0 + u * (-1.0 / 6 + u * (1.0 / 120 + u * (-1.0 / 5040))))
    travel = a >= 0.0
    scale = 1.0 / (N * N)
    h_ref[k1] = jnp.where(travel, cos, jnp.exp(-z)) * scale
    h_ref[4 + k1] = jnp.where(travel, -sin, 0.0) * scale


MESH = pl.DeviceIdType.MESH
ORDER_Z = (2, 3, 1, 0)


def mega(sc_ref, src_h, rcv_h, vel_h, fh_h, fl_h, twy_h, twx_h, img_o, so_o, ro_o, *scr):
    (src, rcv, vel, fh, fl, twy, twx, send1, recv1, send2, recv2, send3, recv3, send4, recv4,
     bh, bl, gx, ht, v1, vp, v2, pk, v4, vf, hdn, hup, htop, hbot, ibuf, ia, ip, ib, im1, i3, oimg,
     so, ro) = scr[:38]
    y_c, y_e = scr[38:44], scr[44:47] + scr[41:44]
    lsem, r1, r2, r3, r4, s1, s2, s3, s4, rv, sv, ri, si, osem = scr[47:]
    freq, me = lax.axis_index("freq"), lax.axis_index("strip")
    x, zhi = freq // 2, freq % 2
    h, s16, zl, yc = me // 16, me % 16, me // 8, me % 8
    ang0, ang1 = sc_ref[8], sc_ref[9]
    ang_h = sc_ref[10]

    ins = [
        pltpu.make_async_copy(a, b, lsem.at[i])
        for i, (a, b) in enumerate(
            [(vel_h, vel), (src_h, src), (rcv_h, rcv), (fh_h, fh), (fl_h, fl), (twy_h, twy), (twx_h, twx)]
        )
    ]
    for c in ins:
        c.start()
    bar = pltpu.get_barrier_semaphore()
    for m in range(1, 32):
        pl.semaphore_signal(bar, inc=1, device_id={"freq": freq, "strip": me ^ m}, device_id_type=MESH)
    for m in range(1, 8):
        pl.semaphore_signal(bar, inc=1, device_id={"freq": freq ^ m, "strip": me}, device_id_type=MESH)
    pl.semaphore_signal(bar, inc=1, device_id={"freq": freq ^ 1, "strip": me ^ 16}, device_id_type=MESH)
    pl.semaphore_wait(bar, 39)

    def remote(a, b, ss, rs, f, s):
        return pltpu.make_async_remote_copy(
            src_ref=a, dst_ref=b, send_sem=ss, recv_sem=rs,
            device_id={"freq": f, "strip": s}, device_id_type=MESH,
        )

    small = []

    def small_send(a, b, ss, rs, f, s):
        c = remote(a, b, ss, rs, f, s)
        c.start()
        small.append(c)

    def arrived(b, rs):
        remote(b, b, rs, rs, freq, me).wait_recv()

    def xpeer(k):
        return lax.rem(x + k, 4)

    ins[0].wait()
    for k in range(1, 4):
        small_send(
            vel.at[0, pl.ds(pl.multiple_of(8 * xpeer(k), 8), 8), :], v1.at[k - 1],
            sv.at[k - 1], rv.at[k - 1], 2 * xpeer(k) + zhi, me,
        )
    for c in ins[1:6]:
        c.wait()

    tw = twy[...]
    for m in ORDER_Z:
        combo = zl ^ m
        phase_a(src, rcv, send1, combo, fh, fl, tw)
        for j in range(8):
            d = combo * 8 + (yc ^ j)
            if m == 0 and j == 0:
                pltpu.make_async_copy(send1.at[d], recv1.at[me], r1.at[me]).start()
            else:
                remote(send1.at[d], recv1.at[me], s1, r1.at[me], freq, d).start()

    for k in range(1, 4):
        arrived(v1.at[k - 1], rv.at[k - 1])
    for d in range(DEPTHS):
        acc = sc_ref[4 * d] * vel[0, pl.ds(pl.multiple_of(8 * x, 8), 8), :]
        for k in range(1, 4):
            acc = acc + sc_ref[4 * d + k] * v1[k - 1]
        vp[d] = acc
    small_send(vp, v2, sv.at[3], rv.at[3], freq ^ 1, me)
    transfer_rows(ht, 0, ang_h, yc)
    transfer_rows(ht, 1, ang_h, yc)
    arrived(v2, rv.at[3])
    pk[0] = vp[0] + v2[0]
    pk[1] = vp[1] + v2[1]
    small_send(pk.at[0], pk.at[2], sv.at[4], rv.at[4], freq, me ^ 16)
    transfer_rows(ht, 2, ang_h, yc)
    transfer_rows(ht, 3, ang_h, yc)
    arrived(pk.at[2], rv.at[4])
    for k in range(1, 4):
        small_send(pk, v4.at[k - 1], sv.at[4 + k], rv.at[4 + k], 2 * xpeer(k) + zhi, me)
    vf[:, pl.ds(pl.multiple_of(8 * x, 8), 8), :] = pk[...]
    for k in range(1, 4):
        arrived(v4.at[k - 1], rv.at[4 + k])
        vf[:, pl.ds(pl.multiple_of(8 * xpeer(4 - k), 8), 8), :] = v4[k - 1]
    hdn[...] = jnp.zeros_like(hdn)
    hup[...] = jnp.zeros_like(hup)
    for d in range(2):
        hdn[d : d + 1, :] = vf[d, 31:32, :]
        hup[d : d + 1, :] = vf[d, 0:1, :]
    below, above = lax.rem(me + 1, 32), lax.rem(me + 31, 32)
    small_send(hdn, htop.at[0], sv.at[8], rv.at[8], freq, below)
    small_send(hdn, htop.at[1], sv.at[9], rv.at[9], freq, below ^ 16)
    small_send(hup, hbot.at[0], sv.at[10], rv.at[10], freq, above)
    small_send(hup, hbot.at[1], sv.at[11], rv.at[11], freq, above ^ 16)

    ins[6].wait()

    def ready1(s8):
        for n1 in range(4):
            arrived(recv1.at[8 * n1 + s8], r1.at[8 * n1 + s8])

    phase_b(
        ready1,
        lambda n1, s8: (recv1[8 * n1 + s8, 0:32, :], recv1[8 * n1 + s8, 32:64, :]),
        store_16(send2), ht, fh, fl, twx, bh, bl, gx,
    )
    for m in range(16):
        d = s16 ^ m
        if m == 0:
            pltpu.make_async_copy(send2.at[d], recv2.at[s16], r2.at[s16]).start()
        else:
            remote(send2.at[d], recv2.at[s16], s2, r2.at[s16], freq, 16 * h + d).start()

    for i, b in enumerate((htop.at[0], htop.at[1], hbot.at[0], hbot.at[1])):
        arrived(b, rv.at[8 + i])

    def ready2(k):
        for p in range(2):
            for half in range(2):
                i = 8 * p + 2 * k + half
                arrived(recv2.at[i], r2.at[i])

    def sent3(t):
        for m in range(16):
            d = s16 ^ m
            if m == 0:
                pltpu.make_async_copy(send3.at[t, d], recv3.at[t, s16], r3.at[t, s16]).start()
            else:
                remote(send3.at[t, d], recv3.at[t, s16], s3.at[t], r3.at[t, s16], freq, 16 * h + d).start()

    phase_c(ready2, sent3, recv2, vf, htop, hbot, h, ang_h, send3, ibuf, y_c, (fh, fl, twy))
    for k in range(1, 4):
        small_send(
            ibuf.at[:, :, pl.ds(pl.multiple_of(256 * xpeer(k), 256), 256)], ia.at[k - 1],
            si.at[k - 1], ri.at[k - 1], 2 * xpeer(k) + zhi, me,
        )

    def ready3(s8):
        for t in range(2):
            for i in (s8, 8 + s8):
                arrived(recv3.at[t, i], r3.at[t, i])

    def load3(n1, s8):
        t, i = n1 // 2, 8 * (n1 % 2) + s8
        return recv3[t, i, 0:32, :], recv3[t, i, 32:64, :]

    phase_b(ready3, load3, store_32(send4), ht, fh, fl, twx, bh, bl, gx)
    for m in ORDER_Z:
        for j in range(8):
            d = me ^ (8 * m + j)
            if m == 0 and j == 0:
                pltpu.make_async_copy(send4.at[d], recv4.at[me], r4.at[me]).start()
            else:
                remote(send4.at[d], recv4.at[me], s4, r4.at[me], freq, d).start()

    for k in range(1, 4):
        arrived(ia.at[k - 1], ri.at[k - 1])
    for t in range(2):
        acc = ibuf[t, :, pl.ds(pl.multiple_of(256 * x, 256), 256)]
        for k in range(3):
            acc = acc + ia[k, t]
        ip[t, 0] = acc[:, 0:128]
        ip[t, 1] = acc[:, 128:256]
    for i, (a, b) in enumerate(((0, 1), (1, 0), (1, 1))):
        small_send(
            ip.at[h ^ b, zhi ^ a], ib.at[i], si.at[3 + i], ri.at[3 + i], freq ^ a, me ^ (16 * b)
        )

    def ready4(k):
        for i in range(4):
            for half in range(2):
                j = 8 * i + 2 * k + half
                arrived(recv4.at[j], r4.at[j])

    outs = []

    def done(f):
        for i, (a, b) in enumerate(((so, so_o), (ro, ro_o))):
            c = pltpu.make_async_copy(a.at[:, f], b.at[:, f], osem.at[2 * f + i])
            c.start()
            outs.append(c)

    phase_e(ready4, done, recv4, vf[1], htop, hbot, (ang0, ang1), so, ro, im1, y_e, (fh, fl, twy))

    for k in range(1, 8):
        small_send(
            im1.at[:, pl.ds(pl.multiple_of(128 * (freq ^ k), 128), 128)], i3.at[k - 1],
            si.at[5 + k], ri.at[5 + k], freq ^ k, me,
        )
    for i in range(3):
        arrived(ib.at[i], ri.at[3 + i])
    oimg[0] = ip[h, zhi] + ib[0] + ib[1] + ib[2]
    remote(send1.at[pl.ds(0, 31)], send1.at[pl.ds(0, 31)], s1, s1, freq, me).wait_send()
    remote(send2.at[pl.ds(0, 15)], send2.at[pl.ds(0, 15)], s2, s2, freq, me).wait_send()
    for t in range(2):
        remote(send3.at[t, pl.ds(0, 15)], send3.at[t, pl.ds(0, 15)], s3.at[t], s3.at[t], freq, me).wait_send()
    remote(send4.at[pl.ds(0, 31)], send4.at[pl.ds(0, 31)], s4, s4, freq, me).wait_send()
    acc = im1[:, pl.ds(pl.multiple_of(128 * freq, 128), 128)]
    for k in range(1, 8):
        arrived(i3.at[k - 1], ri.at[5 + k])
        acc = acc + i3[k - 1]
    oimg[1] = acc
    c = pltpu.make_async_copy(oimg, img_o, osem.at[4])
    c.start()
    outs.append(c)
    for c in small:
        c.wait_send()
    for c in outs:
        c.wait()


def vm(*shape, dtype=F32):
    return pltpu.VMEM(shape, dtype)


def dma(*shape):
    return pltpu.SemaphoreType.DMA(shape)


SCRATCH = [
    vm(2, 2, 32, N), vm(2, 2, 32, N), vm(1, 32, N),
    vm(2 * Q, Q, dtype=BF16), vm(2 * Q, Q, dtype=BF16), vm(8, Q), vm(6, Q, 128),
    vm(32, 64, 128), vm(32, 64, 128), vm(16, 136, 128), vm(16, 136, 128),
    vm(2, 16, 64, 128), vm(2, 16, 64, 128), vm(32, 72, 128), vm(32, 72, 128),
    vm(4, Q, Q, dtype=BF16), vm(4, Q, Q, dtype=BF16), vm(4, Q, Q), vm(8, Q, 128),
    vm(3, 8, N), vm(2, 8, N), vm(2, 8, N), vm(3, 8, N), vm(3, 3, 8, N), vm(3, 32, N),
    vm(8, N), vm(8, N), vm(2, 8, N), vm(2, 8, N),
    vm(2, 32, N), vm(3, 2, 32, 256), vm(2, 2, 32, 128), vm(3, 32, 128), vm(32, N), vm(7, 32, 128),
    vm(2, 32, 128), vm(2, 2, 32, N), vm(2, 2, 32, N),
    vm(272, Q), vm(272, Q), vm(4, 272, Q), vm(4, 48, N), vm(16, N), vm(8, N),
    vm(288, Q), vm(288, Q), vm(4, 288, Q),
    dma(7), dma(32), dma(16), dma(2, 16), dma(32), dma(), dma(), dma(2), dma(),
    dma(12), dma(12), dma(13), dma(13), dma(5),
]


def local(source_field, receiver_field, velocity, slice_owner):
    hi, lo, twy_np = host_tables()
    fh, fl, twy = jnp.asarray(hi), jnp.asarray(lo), jnp.asarray(twy_np)
    twx = jnp.broadcast_to(
        jnp.asarray(np.concatenate([twy_np[1:4], twy_np[5:8]], 0))[:, :, None], (6, Q, 128)
    )
    freq, strip = lax.axis_index("freq"), lax.axis_index("strip")
    ang = [omega_top * (2 * freq + f + 1).astype(F32) / 16 for f in range(2)]
    ang_h = jnp.where(strip < 16, ang[0], ang[1])
    k = jnp.arange(4, dtype=jnp.int32)
    sel = (slice_owner[:DEPTHS, None] == (freq - 2 * k)[None, :] % 8).astype(F32).reshape(8)
    scalars = jnp.concatenate([sel, jnp.stack([ang[0], ang[1], ang_h]), jnp.zeros((5,), F32)])
    any_ = pl.BlockSpec(memory_space=pl.ANY)
    img, so, ro = pl.pallas_call(
        mega,
        out_shape=[
            jax.ShapeDtypeStruct((2, 32, 128), F32),
            jax.ShapeDtypeStruct((2, 2, 32, N), F32),
            jax.ShapeDtypeStruct((2, 2, 32, N), F32),
        ],
        in_specs=[pl.BlockSpec(memory_space=pltpu.SMEM)] + [any_] * 7,
        out_specs=[any_] * 3,
        scratch_shapes=SCRATCH,
        compiler_params=pltpu.CompilerParams(
            collective_id=0, has_side_effects=True, vmem_limit_bytes=56 << 20
        ),
        name="continuation",
    )(scalars, source_field, receiver_field, velocity, fh, fl, twy, twx)
    return img, so, ro


def solution(mesh):
    return jax.shard_map(
        local,
        mesh=mesh,
        in_specs=(
            P(None, "freq", "strip", None),
            P(None, "freq", "strip", None),
            P("freq", "strip", None),
            P(),
        ),
        out_specs=(
            P(None, "strip", "freq"),
            P(None, "freq", "strip", None),
            P(None, "freq", "strip", None),
        ),
        check_vma=False,
    )
```

```python
import functools
import math

import jax
import jax.numpy as jnp
import numpy as np
from jax import lax
from jax.experimental import pallas as pl
from jax.experimental.pallas import tpu as pltpu
from jax.sharding import PartitionSpec as P

DEPTHS = 2
N = 1024
Q = 256
step_length = 0.15
omega_top = 1.2
stencil_gain = 0.05
stencil_damping = 0.1
F32 = jnp.float32
BF16 = jnp.bfloat16


def host_tables():
    i = np.arange(Q)
    ang = 2.0 * np.pi * ((i[:, None] * i[None, :]) % Q) / Q
    cs = np.concatenate([np.cos(ang), np.sin(ang)], 0).astype(np.float32)
    hi = cs.astype(jnp.bfloat16)
    lo = (cs - hi.astype(np.float32)).astype(jnp.bfloat16)
    k = np.arange(4)
    tang = 2.0 * np.pi * (k[:, None] * i[None, :]) / N
    twy = np.concatenate([np.cos(tang), np.sin(tang)], 0).astype(np.float32)
    return hi, lo, twy


def split(x):
    hi = x.astype(BF16)
    lo = (x - hi.astype(F32)).astype(BF16)
    return hi, lo


def mm(a, b):
    return jnp.dot(a, b, preferred_element_type=F32)


def radix4(x, sign):
    (ar, ai), (br, bi), (cr, ci), (dr, di) = x
    t0r, t0i, t1r, t1i = ar + cr, ai + ci, ar - cr, ai - ci
    t2r, t2i, t3r, t3i = br + dr, bi + di, br - dr, bi - di
    o0 = (t0r + t2r, t0i + t2i)
    o2 = (t0r - t2r, t0i - t2i)
    minus = (t1r + t3i, t1i - t3r)
    plus = (t1r - t3i, t1i + t3r)
    return (o0, minus, o2, plus) if sign < 0 else (o0, plus, o2, minus)


def forward_y(xr, xi, fh, fl, twy):
    rows = xr.shape[0]
    parts = [(xr[:, Q * n : Q * n + Q], xi[:, Q * n : Q * n + Q]) for n in range(4)]
    b = radix4(parts, -1)
    stack = []
    for k in range(4):
        r, m = b[k]
        if k:
            c, s = twy[k : k + 1, :], twy[4 + k : 5 + k, :]
            r, m = r * c + m * s, m * c - r * s
        stack += [r, m]
    hi, lo = split(jnp.concatenate(stack, 0))
    pc = mm(hi, fh[:Q]) + mm(lo, fh[:Q]) + mm(hi, fl[:Q])
    ps = mm(hi, fh[Q:]) + mm(lo, fh[Q:]) + mm(hi, fl[Q:])
    out = []
    for k in range(4):
        a, z, e = 2 * k * rows, (2 * k + 1) * rows, (2 * k + 2) * rows
        out.append((pc[a:z] + ps[z:e], pc[z:e] - ps[a:z]))
    return out


def phase_a(src_ref, rcv_ref, send_ref, combo, fh_ref, fl_ref, twy):
    f, p = combo // 2, combo % 2
    first = p == 0
    xr = jnp.where(first, src_ref[0, f], rcv_ref[0, f])
    xi = jnp.where(first, src_ref[1, f], -rcv_ref[1, f])
    out = forward_y(xr, xi, fh_ref[...], fl_ref[...], twy)
    for k in range(4):
        for half in range(2):
            d = combo * 8 + 2 * k + half
            send_ref[d, 0:32, :] = out[k][0][:, 128 * half : 128 * half + 128]
            send_ref[d, 32:64, :] = out[k][1][:, 128 * half : 128 * half + 128]


def phase_b(ready, load, store, h_ref, fh_ref, fl_ref, twx_ref, bh_ref, bl_ref, g_ref):
    for s8 in range(8):
        ready(s8)
        x = radix4([load(n1, s8) for n1 in range(4)], -1)
        sl = slice(32 * s8, 32 * s8 + 32)
        for k in range(4):
            r, m = x[k]
            if k:
                c, s = twx_ref[k - 1, sl, :], twx_ref[2 + k, sl, :]
                r, m = r * c + m * s, m * c - r * s
            rh, rl = split(r)
            mh, ml = split(m)
            bh_ref[k, sl, 0:128] = rh
            bl_ref[k, sl, 0:128] = rl
            bh_ref[k, sl, 128:256] = mh
            bl_ref[k, sl, 128:256] = ml
    for k in range(4):
        fh, fl = fh_ref[...], fl_ref[...]
        bh = bh_ref[k]
        pr = mm(fh, bh) + mm(fl, bh) + mm(fh, bl_ref[k])
        re = pr[:Q, :128] + pr[Q:, 128:]
        im = pr[:Q, 128:] - pr[Q:, :128]
        hr, hi_ = h_ref[k], h_ref[4 + k]
        zr = re * hr - im * hi_
        zi = re * hi_ + im * hr
        zh, zl = split(jnp.concatenate([zr, zi], 1))
        pr = mm(fh, zh) + mm(fl, zh) + mm(fh, zl)
        re = pr[:Q, :128] - pr[Q:, 128:]
        im = pr[:Q, 128:] + pr[Q:, :128]
        if k:
            c, s = twx_ref[k - 1], twx_ref[2 + k]
            re, im = re * c - im * s, im * c + re * s
        g_ref[k, :, 0:128] = re
        g_ref[k, :, 128:256] = im
    for s8 in range(8):
        sl = slice(32 * s8, 32 * s8 + 32)
        x = radix4([(g_ref[k, sl, 0:128], g_ref[k, sl, 128:256]) for k in range(4)], 1)
        for n1 in range(4):
            store(8 * n1 + s8, *x[n1])


def store_16(send_ref):
    zero = jnp.zeros((1, 128), F32)

    def store(s, re, im):
        d, t = s % 16, s // 16
        send_ref[d, 64 * t : 64 * t + 32, :] = re
        send_ref[d, 64 * t + 32 : 64 * t + 64, :] = im
        if s < 31:
            d, t = (s + 1) % 16, (s + 1) // 16
            send_ref[d, 128 + 2 * t : 129 + 2 * t, :] = re[31:32]
            send_ref[d, 132 + 2 * t : 133 + 2 * t, :] = im[31:32]
        else:
            send_ref[15, 131:132, :] = zero
            send_ref[15, 135:136, :] = zero
        if s > 0:
            d, t = (s - 1) % 16, (s - 1) // 16
            send_ref[d, 129 + 2 * t : 130 + 2 * t, :] = re[0:1]
            send_ref[d, 133 + 2 * t : 134 + 2 * t, :] = im[0:1]
        else:
            send_ref[0, 128:129, :] = zero
            send_ref[0, 132:133, :] = zero

    return store


def store_32(send_ref):
    zero = jnp.zeros((1, 128), F32)

    def store(s, re, im):
        send_ref[s, 0:32, :] = re
        send_ref[s, 32:64, :] = im
        if s < 31:
            send_ref[s + 1, 64:65, :] = re[31:32]
            send_ref[s + 1, 66:67, :] = im[31:32]
        else:
            send_ref[31, 65:66, :] = zero
            send_ref[31, 67:68, :] = zero
        send_ref[s, 68:72, :] = jnp.zeros((4, 128), F32)
        if s > 0:
            send_ref[s - 1, 65:66, :] = re[0:1]
            send_ref[s - 1, 67:68, :] = im[0:1]
        else:
            send_ref[0, 64:65, :] = zero
            send_ref[0, 66:67, :] = zero

    return store


def inverse_y(ready, blocks, pairs, fh_ref, fl_ref, twy, pc_ref, ps_ref, g_ref):
    for k in range(4):
        ready(k)
        x = jnp.concatenate([blocks(k, 0), blocks(k, 1)], 1)
        hi, lo = split(x)
        pc_ref[...] = mm(hi, fh_ref[:Q]) + mm(lo, fh_ref[:Q]) + mm(hi, fl_ref[:Q])
        ps_ref[...] = mm(hi, fh_ref[Q:]) + mm(lo, fh_ref[Q:]) + mm(hi, fl_ref[Q:])
        for a, b, n in pairs:
            re = pc_ref[a : a + n] - ps_ref[b : b + n]
            im = pc_ref[b : b + n] + ps_ref[a : a + n]
            if k:
                c, s = twy[k : k + 1, :], twy[4 + k : 5 + k, :]
                re, im = re * c - im * s, im * c + re * s
            g_ref[k, a : a + n, :] = re
            g_ref[k, b : b + n, :] = im


def corrected(g_ref, a, b, n, rot):
    x = radix4([(g_ref[k, a : a + n, :], g_ref[k, b : b + n, :]) for k in range(4)], 1)
    re = jnp.concatenate([x[i][0] for i in range(4)], 1)
    im = jnp.concatenate([x[i][1] for i in range(4)], 1)
    c, s = rot
    return re * c + im * s, im * c - re * s


def rotation(speed, angular):
    ph = angular * step_length * (1.0 / speed - 1.0)
    u = ph * ph
    c = 1.0 + u * (-0.5 + u * (1.0 / 24 + u * (-1.0 / 720)))
    s = ph * (1.0 + u * (-1.0 / 6 + u * (1.0 / 120 + u * (-1.0 / 5040))))
    return c, s


def laplace(ref, idx, lane):
    mid = ref[idx, 8:40, :]
    left = jnp.where(lane == 0, 0.0, pltpu.roll(mid, 1, 1))
    right = jnp.where(lane == N - 1, 0.0, pltpu.roll(mid, N - 1, 1))
    beside = ref[idx, 9:41, :] + ref[idx, 7:39, :]
    return mid, beside + left + right - 4.0 * mid


def continued(fld_ref, i, weight, lane):
    pr, lr = laplace(fld_ref, 2 * i, lane)
    pi_, li = laplace(fld_ref, 2 * i + 1, lane)
    return (
        pr + weight * (stencil_damping * lr + li),
        pi_ + weight * (stencil_damping * li - lr),
    )


def weight_of(speed, angular):
    return stencil_gain * (speed * speed - 1.0) * angular / omega_top


def phase_c(ready, sent, recv_ref, vel_ref, htop_ref, hbot_ref, h, angular, send_ref, img_ref, scr, tabs):
    fh_ref, fl_ref, twy_ref = tabs
    pc_ref, ps_ref, g_ref, fld_ref, tmp_ref, hv_ref = scr
    twy = twy_ref[...]
    pairs = []
    for p in range(2):
        o = 136 * p
        pairs += [(o, o + 32, 32), (o + 64, o + 96, 32), (o + 128, o + 132, 4)]

    def blocks(k, half):
        return jnp.concatenate([recv_ref[2 * k + half], recv_ref[8 + 2 * k + half]], 0)

    inverse_y(ready, blocks, pairs, fh_ref, fl_ref, twy, pc_ref, ps_ref, g_ref)
    lane = lax.broadcasted_iota(jnp.int32, (32, N), 1)
    for t in range(2):
        own = h == t
        hv_ref[2 * t : 2 * t + 1, :] = jnp.where(own, htop_ref[0, 0:1, :], htop_ref[1, 0:1, :])
        hv_ref[2 * t + 1 : 2 * t + 2, :] = jnp.where(own, hbot_ref[0, 0:1, :], hbot_ref[1, 0:1, :])
    hrot = rotation(hv_ref[0:4, :], angular)
    for p in range(2):
        o = 136 * p + 128
        re, im = corrected(g_ref, o, o + 4, 4, hrot)
        tmp_ref[4 * p : 4 * p + 4, :] = re
        tmp_ref[8 + 4 * p : 12 + 4 * p, :] = im
    for t in range(2):
        speed = jnp.where(h == t, vel_ref[0], vel_ref[1])
        rot = rotation(speed, angular)
        weight = weight_of(speed, angular)
        outs = []
        for p in range(2):
            o = 136 * p + 64 * t
            re, im = corrected(g_ref, o, o + 32, 32, rot)
            fld_ref[2 * p, 8:40, :] = re
            fld_ref[2 * p + 1, 8:40, :] = im
            for c in range(2):
                r = 8 * c + 4 * p + 2 * t
                fld_ref[2 * p + c, 7:8, :] = tmp_ref[r : r + 1, :]
                fld_ref[2 * p + c, 40:41, :] = tmp_ref[r + 1 : r + 2, :]
            re, im = continued(fld_ref, p, weight, lane)
            outs.append((re, im))
            out = forward_y(re, im, fh_ref[...], fl_ref[...], twy)
            for k in range(4):
                for half in range(2):
                    d = p * 8 + 2 * k + half
                    ls = slice(128 * half, 128 * half + 128)
                    send_ref[t, d, 0:32, :] = out[k][0][:, ls]
                    send_ref[t, d, 32:64, :] = out[k][1][:, ls]
        sent(t)
        img_ref[t] = outs[0][0] * outs[1][0] - outs[0][1] * outs[1][1]


def phase_e(ready, done, recv_ref, speed, htop_ref, hbot_ref, angulars, src_ref, rcv_ref, img_ref, scr, tabs):
    fh_ref, fl_ref, twy_ref = tabs
    pc_ref, ps_ref, g_ref, fld_ref, tmp_ref, hv_ref = scr
    twy = twy_ref[...]
    pairs = []
    for i in range(4):
        o = 72 * i
        pairs += [(o, o + 32, 32), (o + 64, o + 66, 2)]

    def blocks(k, half):
        return jnp.concatenate([recv_ref[8 * i + 2 * k + half] for i in range(4)], 0)

    inverse_y(ready, blocks, pairs, fh_ref, fl_ref, twy, pc_ref, ps_ref, g_ref)
    lane = lax.broadcasted_iota(jnp.int32, (32, N), 1)
    hv_ref[0:1, :] = htop_ref[2, 0:1, :]
    hv_ref[1:2, :] = hbot_ref[2, 0:1, :]
    for f in range(2):
        rot = rotation(speed, angulars[f])
        hrot = rotation(hv_ref[0:2, :], angulars[f])
        weight = weight_of(speed, angulars[f])
        outs = []
        for p in range(2):
            o = 72 * (2 * f + p)
            re, im = corrected(g_ref, o + 64, o + 66, 2, hrot)
            tmp_ref[0:2, :] = re
            tmp_ref[8:10, :] = im
            re, im = corrected(g_ref, o, o + 32, 32, rot)
            fld_ref[2 * p, 8:40, :] = re
            fld_ref[2 * p + 1, 8:40, :] = im
            for c in range(2):
                fld_ref[2 * p + c, 7:8, :] = tmp_ref[8 * c : 8 * c + 1, :]
                fld_ref[2 * p + c, 40:41, :] = tmp_ref[8 * c + 1 : 8 * c + 2, :]
            re, im = continued(fld_ref, p, weight, lane)
            outs.append((re, im))
            ref = (src_ref, rcv_ref)[p]
            ref[0, f] = re
            ref[1, f] = -im if p else im
        term = outs[0][0] * outs[1][0] - outs[0][1] * outs[1][1]
        img_ref[...] = img_ref[...] + term if f else term
        done(f)


def centered(position):
    shifted = jnp.where(position < N // 2, position, position - N)
    return shifted.astype(F32) * (2.0 * math.pi / N)


def transfer_rows(h_ref, k1, angular, yc):
    k2 = lax.broadcasted_iota(jnp.int32, (Q, 128), 0)
    lane = lax.broadcasted_iota(jnp.int32, (Q, 128), 1)
    wx = centered(4 * k2 + k1)
    wy = centered(4 * ((yc % 2) * 128 + lane) + yc // 2)
    a = angular * angular - (wx * wx + wy * wy)
    z = step_length * jnp.sqrt(jnp.abs(a))
    u = z * z
    cos = 1.0 + u * (-0.5 + u * (1.0 / 24 + u * (-1.0 / 720 + u * (1.0 / 40320))))
    sin = z * (1.0 + u * (-1.0 / 6 + u * (1.0 / 120 + u * (-1.0 / 5040))))
    travel = a >= 0.0
    scale = 1.0 / (N * N)
    h_ref[k1] = jnp.where(travel, cos, jnp.exp(-z)) * scale
    h_ref[4 + k1] = jnp.where(travel, -sin, 0.0) * scale


MESH = pl.DeviceIdType.MESH
ORDER_Z = (2, 3, 1, 0)


def mega(owner_ref, src_h, rcv_h, vel_h, fh_h, fl_h, twy_h, twx_h, oimg, so, ro, *scr):
    (src, rcv, vel, fh, fl, twy, twx, send1, recv1, send2, recv2, send3, recv3, send4, recv4,
     bh, bl, gx, ht, v1, vp, v2, pk, v4, vf, hdn, hup, htop, hbot, ibuf, ia, ip, ib, im1, i3, v3) = scr[:36]
    y_c, y_e = scr[36:42], scr[42:45] + scr[39:42]
    lsem, r1, r2, r3, r4, s1, s2, s3, s4, rv, sv, ri, si = scr[45:]
    freq, me = lax.axis_index("freq"), lax.axis_index("strip")
    x, zhi = freq // 2, freq % 2
    h, s16, zl, yc = me // 16, me % 16, me // 8, me % 8
    ang0 = omega_top * (2 * freq + 1).astype(F32) / 16
    ang1 = omega_top * (2 * freq + 2).astype(F32) / 16
    ang_h = jnp.where(h == 0, ang0, ang1)

    ins = [
        pltpu.make_async_copy(a, b, lsem.at[i])
        for i, (a, b) in enumerate(
            [(vel_h, vel), (src_h, src), (rcv_h, rcv), (fh_h, fh), (fl_h, fl), (twy_h, twy), (twx_h, twx)]
        )
    ]
    for c in ins:
        c.start()
    bar = pltpu.get_barrier_semaphore()
    for m in range(1, 32):
        pl.semaphore_signal(bar, inc=1, device_id={"freq": freq, "strip": me ^ m}, device_id_type=MESH)
    for m in range(1, 8):
        pl.semaphore_signal(bar, inc=1, device_id={"freq": freq ^ m, "strip": me}, device_id_type=MESH)
    pl.semaphore_signal(bar, inc=1, device_id={"freq": freq ^ 1, "strip": me ^ 16}, device_id_type=MESH)

    def remote(a, b, ss, rs, f, s):
        return pltpu.make_async_remote_copy(
            src_ref=a, dst_ref=b, send_sem=ss, recv_sem=rs,
            device_id={"freq": f, "strip": s}, device_id_type=MESH,
        )

    small = []

    def small_send(a, b, ss, rs, f, s):
        c = remote(a, b, ss, rs, f, s)
        c.start()
        small.append(c)

    def arrived(b, rs):
        remote(b, b, rs, rs, freq, me).wait_recv()

    def xpeer(k):
        return lax.rem(x + k, 4)

    def send_1(m):
        combo = zl ^ m
        for j in range(8):
            d = combo * 8 + (yc ^ j)
            if m == 0 and j == 0:
                pltpu.make_async_copy(send1.at[d], recv1.at[me], r1.at[me]).start()
            else:
                remote(send1.at[d], recv1.at[me], s1, r1.at[me], freq, d).start()

    for c in ins[:6]:
        c.wait()
    tw = twy[...]
    phase_a(src, rcv, send1, zl, fh, fl, tw)
    phase_a(src, rcv, send1, zl ^ 1, fh, fl, tw)
    pl.semaphore_wait(bar, 39)

    for k in range(1, 4):
        small_send(
            vel.at[0, pl.ds(pl.multiple_of(8 * xpeer(k), 8), 8), :], v1.at[k - 1],
            sv.at[k - 1], rv.at[k - 1], 2 * xpeer(k) + zhi, me,
        )
    send_1(0)
    phase_a(src, rcv, send1, zl ^ 2, fh, fl, tw)
    phase_a(src, rcv, send1, zl ^ 3, fh, fl, tw)

    for k in range(1, 4):
        arrived(v1.at[k - 1], rv.at[k - 1])
    for d in range(DEPTHS):
        acc = 0.0
        for k in range(4):
            take = jnp.where(owner_ref[d] == lax.rem(freq + 8 - 2 * k, 8), 1.0, 0.0)
            rows = v1[k - 1] if k else vel[0, pl.ds(pl.multiple_of(8 * x, 8), 8), :]
            acc = acc + take * rows
        vp[d] = acc
    small_send(vp.at[0], v2.at[0], sv.at[3], rv.at[3], freq ^ 1, me)
    small_send(vp.at[0], v3.at[0], sv.at[4], rv.at[4], freq, me ^ 16)
    small_send(vp.at[0], v3.at[1], sv.at[12], rv.at[12], freq ^ 1, me ^ 16)
    send_1(2)
    send_1(3)
    send_1(1)
    for k in range(4):
        transfer_rows(ht, k, ang_h, yc)
    arrived(v2.at[0], rv.at[3])
    arrived(v3.at[0], rv.at[4])
    arrived(v3.at[1], rv.at[12])
    pk[0] = vp[0] + v2[0]
    pk[1] = v3[0] + v3[1]
    two = pl.ds(0, 2)
    for k in range(1, 4):
        small_send(pk.at[two], v4.at[k - 1, two], sv.at[4 + k], rv.at[4 + k], 2 * xpeer(k) + zhi, me)
    vf[0:2, pl.ds(pl.multiple_of(8 * x, 8), 8), :] = pk[0:2]
    for k in range(1, 4):
        arrived(v4.at[k - 1, two], rv.at[4 + k])
        vf[0:2, pl.ds(pl.multiple_of(8 * xpeer(4 - k), 8), 8), :] = v4[k - 1, 0:2]
    hdn[...] = jnp.zeros_like(hdn)
    hup[...] = jnp.zeros_like(hup)
    hdn[0, 0:1, :] = vf[0, 31:32, :]
    hup[0, 0:1, :] = vf[0, 0:1, :]
    below, above = lax.rem(me + 1, 32), lax.rem(me + 31, 32)
    small_send(hdn.at[0], htop.at[0], sv.at[8], rv.at[8], freq, below)
    small_send(hdn.at[0], htop.at[1], sv.at[9], rv.at[9], freq, below ^ 16)
    small_send(hup.at[0], hbot.at[0], sv.at[10], rv.at[10], freq, above)
    small_send(hup.at[0], hbot.at[1], sv.at[11], rv.at[11], freq, above ^ 16)

    ins[6].wait()

    def ready1(s8):
        for n1 in range(4):
            arrived(recv1.at[8 * n1 + s8], r1.at[8 * n1 + s8])

    phase_b(
        ready1,
        lambda n1, s8: (recv1[8 * n1 + s8, 0:32, :], recv1[8 * n1 + s8, 32:64, :]),
        store_16(send2), ht, fh, fl, twx, bh, bl, gx,
    )
    for m in range(16):
        d = s16 ^ m
        if m == 0:
            pltpu.make_async_copy(send2.at[d], recv2.at[s16], r2.at[s16]).start()
        else:
            remote(send2.at[d], recv2.at[s16], s2, r2.at[s16], freq, 16 * h + d).start()

    for i, b in enumerate((htop.at[0], htop.at[1], hbot.at[0], hbot.at[1])):
        arrived(b, rv.at[8 + i])

    def ready2(k):
        for p in range(2):
            for half in range(2):
                i = 8 * p + 2 * k + half
                arrived(recv2.at[i], r2.at[i])
        if k == 3:
            small_send(vp.at[1], v2.at[1], sv.at[13], rv.at[13], freq ^ 1, me)

    def sent3(t):
        for m in range(16):
            d = s16 ^ m
            if m == 0:
                pltpu.make_async_copy(send3.at[t, d], recv3.at[t, s16], r3.at[t, s16]).start()
            else:
                remote(send3.at[t, d], recv3.at[t, s16], s3.at[t], r3.at[t, s16], freq, 16 * h + d).start()

    phase_c(ready2, sent3, recv2, vf, htop, hbot, h, ang_h, send3, ibuf, y_c, (fh, fl, twy))
    for k in range(1, 4):
        small_send(
            ibuf.at[:, :, pl.ds(pl.multiple_of(256 * xpeer(k), 256), 256)], ia.at[k - 1],
            si.at[k - 1], ri.at[k - 1], 2 * xpeer(k) + zhi, me,
        )

    arrived(v2.at[1], rv.at[13])
    pk[2] = vp[1] + v2[1]
    for k in range(1, 4):
        small_send(pk.at[2], v4.at[k - 1, 2], sv.at[13 + k], rv.at[13 + k], 2 * xpeer(k) + zhi, me)

    def ready3(s8):
        for t in range(2):
            for i in (s8, 8 + s8):
                arrived(recv3.at[t, i], r3.at[t, i])

    def load3(n1, s8):
        t, i = n1 // 2, 8 * (n1 % 2) + s8
        return recv3[t, i, 0:32, :], recv3[t, i, 32:64, :]

    phase_b(ready3, load3, store_32(send4), ht, fh, fl, twx, bh, bl, gx)
    vf[2, pl.ds(pl.multiple_of(8 * x, 8), 8), :] = pk[2]
    for k in range(1, 4):
        arrived(v4.at[k - 1, 2], rv.at[13 + k])
        vf[2, pl.ds(pl.multiple_of(8 * xpeer(4 - k), 8), 8), :] = v4[k - 1, 2]
    hdn[1, 0:1, :] = vf[2, 31:32, :]
    hup[1, 0:1, :] = vf[2, 0:1, :]
    small_send(hdn.at[1], htop.at[2], sv.at[17], rv.at[17], freq, below)
    small_send(hup.at[1], hbot.at[2], sv.at[18], rv.at[18], freq, above)
    for m in ORDER_Z:
        for j in range(8):
            d = me ^ (8 * m + j)
            if m == 0 and j == 0:
                pltpu.make_async_copy(send4.at[d, pl.ds(0, 68)], recv4.at[me, pl.ds(0, 68)], r4.at[me]).start()
            else:
                remote(send4.at[d, pl.ds(0, 68)], recv4.at[me, pl.ds(0, 68)], s4, r4.at[me], freq, d).start()

    for k in range(1, 4):
        arrived(ia.at[k - 1], ri.at[k - 1])
    for t in range(2):
        acc = ibuf[t, :, pl.ds(pl.multiple_of(256 * x, 256), 256)]
        for k in range(3):
            acc = acc + ia[k, t]
        ip[t, 0] = acc[:, 0:128]
        ip[t, 1] = acc[:, 128:256]
    for i, (a, b) in enumerate(((0, 1), (1, 0), (1, 1))):
        small_send(
            ip.at[h ^ b, zhi ^ a], ib.at[i], si.at[3 + i], ri.at[3 + i], freq ^ a, me ^ (16 * b)
        )

    def ready4(k):
        for i in range(4):
            for half in range(2):
                j = 8 * i + 2 * k + half
                arrived(recv4.at[j, pl.ds(0, 68)], r4.at[j])

    arrived(htop.at[2], rv.at[17])
    arrived(hbot.at[2], rv.at[18])
    phase_e(ready4, lambda f: None, recv4, vf[2], htop, hbot, (ang0, ang1), so, ro, im1, y_e, (fh, fl, twy))

    for k in range(1, 8):
        small_send(
            im1.at[:, pl.ds(pl.multiple_of(128 * (freq ^ k), 128), 128)], i3.at[k - 1],
            si.at[5 + k], ri.at[5 + k], freq ^ k, me,
        )
    for i in range(3):
        arrived(ib.at[i], ri.at[3 + i])
    oimg[0] = ip[h, zhi] + ib[0] + ib[1] + ib[2]
    remote(send1.at[pl.ds(0, 31)], send1.at[pl.ds(0, 31)], s1, s1, freq, me).wait_send()
    remote(send2.at[pl.ds(0, 15)], send2.at[pl.ds(0, 15)], s2, s2, freq, me).wait_send()
    for t in range(2):
        remote(send3.at[t, pl.ds(0, 15)], send3.at[t, pl.ds(0, 15)], s3.at[t], s3.at[t], freq, me).wait_send()
    remote(send4.at[pl.ds(0, 31), pl.ds(0, 68)], send4.at[pl.ds(0, 31), pl.ds(0, 68)], s4, s4, freq, me).wait_send()
    acc = im1[:, pl.ds(pl.multiple_of(128 * freq, 128), 128)]
    for k in range(1, 8):
        arrived(i3.at[k - 1], ri.at[5 + k])
        acc = acc + i3[k - 1]
    oimg[1] = acc
    for c in small:
        c.wait_send()


def vm(*shape, dtype=F32):
    return pltpu.VMEM(shape, dtype)


def dma(*shape):
    return pltpu.SemaphoreType.DMA(shape)


SCRATCH = [
    vm(2, 2, 32, N), vm(2, 2, 32, N), vm(1, 32, N),
    vm(2 * Q, Q, dtype=BF16), vm(2 * Q, Q, dtype=BF16), vm(8, Q), vm(6, Q, 128),
    vm(32, 64, 128), vm(32, 64, 128), vm(16, 136, 128), vm(16, 136, 128),
    vm(2, 16, 64, 128), vm(2, 16, 64, 128), vm(32, 72, 128), vm(32, 72, 128),
    vm(4, Q, Q, dtype=BF16), vm(4, Q, Q, dtype=BF16), vm(4, Q, Q), vm(8, Q, 128),
    vm(3, 8, N), vm(2, 8, N), vm(2, 8, N), vm(3, 8, N), vm(3, 3, 8, N), vm(3, 32, N),
    vm(2, 8, N), vm(2, 8, N), vm(3, 8, N), vm(3, 8, N),
    vm(2, 32, N), vm(3, 2, 32, 256), vm(2, 2, 32, 128), vm(3, 32, 128), vm(32, N), vm(7, 32, 128),
    vm(2, 8, N),
    vm(272, Q), vm(272, Q), vm(4, 272, Q), vm(4, 48, N), vm(16, N), vm(8, N),
    vm(288, Q), vm(288, Q), vm(4, 288, Q),
    dma(7), dma(32), dma(16), dma(2, 16), dma(32), dma(), dma(), dma(2), dma(),
    dma(19), dma(19), dma(13), dma(13),
]


def put_out(img_i, so_i, ro_i, img_o, so_o, ro_o, img_v, so_v, ro_v, sem_in, sem_out):
    jobs = [(img_i, img_v, img_o)]
    for f in range(4):
        i = (f // 2, f % 2)
        jobs += [(so_i.at[i], so_v.at[i], so_o.at[i]), (ro_i.at[i], ro_v.at[i], ro_o.at[i])]
    loads = [pltpu.make_async_copy(a, b, sem_in.at[n]) for n, (a, b, _) in enumerate(jobs)]
    stores = [pltpu.make_async_copy(b, c, sem_out.at[n]) for n, (_, b, c) in enumerate(jobs)]
    for c in loads:
        c.start()
    for a, b in zip(loads, stores):
        a.wait()
        b.start()
    for c in stores:
        c.wait()


def finish(img, so, ro):
    any_ = pl.BlockSpec(memory_space=pl.ANY)
    return pl.pallas_call(
        put_out,
        out_shape=[jax.ShapeDtypeStruct(a.shape, F32) for a in (img, so, ro)],
        in_specs=[any_] * 3,
        out_specs=[any_] * 3,
        scratch_shapes=[vm(*a.shape) for a in (img, so, ro)] + [dma(9), dma(9)],
        name="put_out",
    )(img, so, ro)


def local(source_field, receiver_field, velocity, slice_owner):
    hi, lo, twy_np = host_tables()
    fh, fl, twy = jnp.asarray(hi), jnp.asarray(lo), jnp.asarray(twy_np)
    twx = jnp.asarray(
        np.ascontiguousarray(
            np.broadcast_to(np.concatenate([twy_np[1:4], twy_np[5:8]], 0)[:, :, None], (6, Q, 128))
        )
    )
    any_ = pl.BlockSpec(memory_space=pl.ANY)
    img, so, ro = pl.pallas_call(
        mega,
        out_shape=[
            jax.ShapeDtypeStruct((2, 32, 128), F32),
            jax.ShapeDtypeStruct((2, 2, 32, N), F32),
            jax.ShapeDtypeStruct((2, 2, 32, N), F32),
        ],
        in_specs=[pl.BlockSpec(memory_space=pltpu.SMEM)] + [any_] * 7,
        out_specs=[pl.BlockSpec(memory_space=pltpu.VMEM)] * 3,
        scratch_shapes=SCRATCH,
        compiler_params=pltpu.CompilerParams(
            collective_id=0, has_side_effects=True, vmem_limit_bytes=62 << 20
        ),
        name="continuation",
    )(slice_owner, source_field, receiver_field, velocity, fh, fl, twy, twx)
    return finish(img, so, ro)


def solution(mesh):
    return jax.shard_map(
        local,
        mesh=mesh,
        in_specs=(
            P(None, "freq", "strip", None),
            P(None, "freq", "strip", None),
            P("freq", "strip", None),
            P(),
        ),
        out_specs=(
            P(None, "strip", "freq"),
            P(None, "freq", "strip", None),
            P(None, "freq", "strip", None),
        ),
        check_vma=False,
    )
```

```python
import functools
import math

import jax
import jax.numpy as jnp
import numpy as np
from jax import lax
from jax.experimental import pallas as pl
from jax.experimental.pallas import tpu as pltpu
from jax.sharding import PartitionSpec as P

DEPTHS = 2
N = 1024
Q = 256
step_length = 0.15
omega_top = 1.2
stencil_gain = 0.05
stencil_damping = 0.1
F32 = jnp.float32
BF16 = jnp.bfloat16


def host_tables():
    i = np.arange(Q)
    ang = 2.0 * np.pi * ((i[:, None] * i[None, :]) % Q) / Q
    cs = np.concatenate([np.cos(ang), np.sin(ang)], 0).astype(np.float32)
    hi = cs.astype(jnp.bfloat16)
    lo = (cs - hi.astype(np.float32)).astype(jnp.bfloat16)
    k = np.arange(4)
    tang = 2.0 * np.pi * (k[:, None] * i[None, :]) / N
    twy = np.concatenate([np.cos(tang), np.sin(tang)], 0).astype(np.float32)
    return hi, lo, twy


def split(x):
    hi = x.astype(BF16)
    lo = (x - hi.astype(F32)).astype(BF16)
    return hi, lo


def mm(a, b):
    return jnp.dot(a, b, preferred_element_type=F32)


def radix4(x, sign):
    (ar, ai), (br, bi), (cr, ci), (dr, di) = x
    t0r, t0i, t1r, t1i = ar + cr, ai + ci, ar - cr, ai - ci
    t2r, t2i, t3r, t3i = br + dr, bi + di, br - dr, bi - di
    o0 = (t0r + t2r, t0i + t2i)
    o2 = (t0r - t2r, t0i - t2i)
    minus = (t1r + t3i, t1i - t3r)
    plus = (t1r - t3i, t1i + t3r)
    return (o0, minus, o2, plus) if sign < 0 else (o0, plus, o2, minus)


def forward_y(xr, xi, fh, fl, twy):
    rows = xr.shape[0]
    parts = [(xr[:, Q * n : Q * n + Q], xi[:, Q * n : Q * n + Q]) for n in range(4)]
    b = radix4(parts, -1)
    stack = []
    for k in range(4):
        r, m = b[k]
        if k:
            c, s = twy[k : k + 1, :], twy[4 + k : 5 + k, :]
            r, m = r * c + m * s, m * c - r * s
        stack += [r, m]
    hi, lo = split(jnp.concatenate(stack, 0))
    pc = mm(hi, fh[:Q]) + mm(lo, fh[:Q]) + mm(hi, fl[:Q])
    ps = mm(hi, fh[Q:]) + mm(lo, fh[Q:]) + mm(hi, fl[Q:])
    out = []
    for k in range(4):
        a, z, e = 2 * k * rows, (2 * k + 1) * rows, (2 * k + 2) * rows
        out.append((pc[a:z] + ps[z:e], pc[z:e] - ps[a:z]))
    return out


def phase_a(src_ref, rcv_ref, send_ref, combo, fh_ref, fl_ref, twy):
    f, p = combo // 2, combo % 2
    first = p == 0
    xr = jnp.where(first, src_ref[0, f], rcv_ref[0, f])
    xi = jnp.where(first, src_ref[1, f], -rcv_ref[1, f])
    out = forward_y(xr, xi, fh_ref[...], fl_ref[...], twy)
    for k in range(4):
        for half in range(2):
            d = combo * 8 + 2 * k + half
            send_ref[d, 0:32, :] = out[k][0][:, 128 * half : 128 * half + 128]
            send_ref[d, 32:64, :] = out[k][1][:, 128 * half : 128 * half + 128]


def phase_b(ready, load, store, h_ref, fh_ref, fl_ref, twx_ref, bh_ref, bl_ref, g_ref):
    for s8 in range(8):
        ready(s8)
        x = radix4([load(n1, s8) for n1 in range(4)], -1)
        sl = slice(32 * s8, 32 * s8 + 32)
        for k in range(4):
            r, m = x[k]
            if k:
                c, s = twx_ref[k - 1, sl, :], twx_ref[2 + k, sl, :]
                r, m = r * c + m * s, m * c - r * s
            rh, rl = split(r)
            mh, ml = split(m)
            bh_ref[k, sl, 0:128] = rh
            bl_ref[k, sl, 0:128] = rl
            bh_ref[k, sl, 128:256] = mh
            bl_ref[k, sl, 128:256] = ml
    for k in range(4):
        fh, fl = fh_ref[...], fl_ref[...]
        bh = bh_ref[k]
        pr = mm(fh, bh) + mm(fl, bh) + mm(fh, bl_ref[k])
        re = pr[:Q, :128] + pr[Q:, 128:]
        im = pr[:Q, 128:] - pr[Q:, :128]
        hr, hi_ = h_ref[k], h_ref[4 + k]
        zr = re * hr - im * hi_
        zi = re * hi_ + im * hr
        zh, zl = split(jnp.concatenate([zr, zi], 1))
        pr = mm(fh, zh) + mm(fl, zh) + mm(fh, zl)
        re = pr[:Q, :128] - pr[Q:, 128:]
        im = pr[:Q, 128:] + pr[Q:, :128]
        if k:
            c, s = twx_ref[k - 1], twx_ref[2 + k]
            re, im = re * c - im * s, im * c + re * s
        g_ref[k, :, 0:128] = re
        g_ref[k, :, 128:256] = im
    for s8 in range(8):
        sl = slice(32 * s8, 32 * s8 + 32)
        x = radix4([(g_ref[k, sl, 0:128], g_ref[k, sl, 128:256]) for k in range(4)], 1)
        for n1 in range(4):
            store(8 * n1 + s8, *x[n1])


def store_16(send_ref):
    zero = jnp.zeros((1, 128), F32)

    def store(s, re, im):
        d, t = s % 16, s // 16
        send_ref[d, 64 * t : 64 * t + 32, :] = re
        send_ref[d, 64 * t + 32 : 64 * t + 64, :] = im
        if s < 31:
            d, t = (s + 1) % 16, (s + 1) // 16
            send_ref[d, 128 + 2 * t : 129 + 2 * t, :] = re[31:32]
            send_ref[d, 132 + 2 * t : 133 + 2 * t, :] = im[31:32]
        else:
            send_ref[15, 131:132, :] = zero
            send_ref[15, 135:136, :] = zero
        if s > 0:
            d, t = (s - 1) % 16, (s - 1) // 16
            send_ref[d, 129 + 2 * t : 130 + 2 * t, :] = re[0:1]
            send_ref[d, 133 + 2 * t : 134 + 2 * t, :] = im[0:1]
        else:
            send_ref[0, 128:129, :] = zero
            send_ref[0, 132:133, :] = zero

    return store


def store_32(send_ref):
    zero = jnp.zeros((1, 128), F32)

    def store(s, re, im):
        send_ref[s, 0:32, :] = re
        send_ref[s, 32:64, :] = im
        if s < 31:
            send_ref[s + 1, 64:65, :] = re[31:32]
            send_ref[s + 1, 66:67, :] = im[31:32]
        else:
            send_ref[31, 65:66, :] = zero
            send_ref[31, 67:68, :] = zero
        send_ref[s, 68:72, :] = jnp.zeros((4, 128), F32)
        if s > 0:
            send_ref[s - 1, 65:66, :] = re[0:1]
            send_ref[s - 1, 67:68, :] = im[0:1]
        else:
            send_ref[0, 64:65, :] = zero
            send_ref[0, 66:67, :] = zero

    return store


def inverse_y(ready, blocks, pairs, fh_ref, fl_ref, twy, pc_ref, ps_ref, g_ref):
    for k in range(4):
        ready(k)
        x = jnp.concatenate([blocks(k, 0), blocks(k, 1)], 1)
        hi, lo = split(x)
        pc_ref[...] = mm(hi, fh_ref[:Q]) + mm(lo, fh_ref[:Q]) + mm(hi, fl_ref[:Q])
        ps_ref[...] = mm(hi, fh_ref[Q:]) + mm(lo, fh_ref[Q:]) + mm(hi, fl_ref[Q:])
        for a, b, n in pairs:
            re = pc_ref[a : a + n] - ps_ref[b : b + n]
            im = pc_ref[b : b + n] + ps_ref[a : a + n]
            if k:
                c, s = twy[k : k + 1, :], twy[4 + k : 5 + k, :]
                re, im = re * c - im * s, im * c + re * s
            g_ref[k, a : a + n, :] = re
            g_ref[k, b : b + n, :] = im


def corrected(g_ref, a, b, n, rot):
    x = radix4([(g_ref[k, a : a + n, :], g_ref[k, b : b + n, :]) for k in range(4)], 1)
    re = jnp.concatenate([x[i][0] for i in range(4)], 1)
    im = jnp.concatenate([x[i][1] for i in range(4)], 1)
    c, s = rot
    return re * c + im * s, im * c - re * s


def rotation(speed, angular):
    ph = angular * step_length * (1.0 / speed - 1.0)
    u = ph * ph
    c = 1.0 + u * (-0.5 + u * (1.0 / 24 + u * (-1.0 / 720)))
    s = ph * (1.0 + u * (-1.0 / 6 + u * (1.0 / 120 + u * (-1.0 / 5040))))
    return c, s


def laplace(ref, idx, lane):
    mid = ref[idx, 8:40, :]
    left = jnp.where(lane == 0, 0.0, pltpu.roll(mid, 1, 1))
    right = jnp.where(lane == N - 1, 0.0, pltpu.roll(mid, N - 1, 1))
    beside = ref[idx, 9:41, :] + ref[idx, 7:39, :]
    return mid, beside + left + right - 4.0 * mid


def continued(fld_ref, i, weight, lane):
    pr, lr = laplace(fld_ref, 2 * i, lane)
    pi_, li = laplace(fld_ref, 2 * i + 1, lane)
    return (
        pr + weight * (stencil_damping * lr + li),
        pi_ + weight * (stencil_damping * li - lr),
    )


def weight_of(speed, angular):
    return stencil_gain * (speed * speed - 1.0) * angular / omega_top


def phase_c(ready, sent, recv_ref, vel_ref, htop_ref, hbot_ref, h, angular, send_ref, img_ref, scr, tabs):
    fh_ref, fl_ref, twy_ref = tabs
    pc_ref, ps_ref, g_ref, fld_ref, tmp_ref, hv_ref = scr
    twy = twy_ref[...]
    pairs = []
    for p in range(2):
        o = 136 * p
        pairs += [(o, o + 32, 32), (o + 64, o + 96, 32), (o + 128, o + 132, 4)]

    def blocks(k, half):
        return jnp.concatenate([recv_ref[2 * k + half], recv_ref[8 + 2 * k + half]], 0)

    inverse_y(ready, blocks, pairs, fh_ref, fl_ref, twy, pc_ref, ps_ref, g_ref)
    ready(4)
    lane = lax.broadcasted_iota(jnp.int32, (32, N), 1)
    for t in range(2):
        own = h == t
        hv_ref[2 * t : 2 * t + 1, :] = jnp.where(own, htop_ref[0, 0:1, :], htop_ref[1, 0:1, :])
        hv_ref[2 * t + 1 : 2 * t + 2, :] = jnp.where(own, hbot_ref[0, 0:1, :], hbot_ref[1, 0:1, :])
    hrot = rotation(hv_ref[0:4, :], angular)
    for p in range(2):
        o = 136 * p + 128
        re, im = corrected(g_ref, o, o + 4, 4, hrot)
        tmp_ref[4 * p : 4 * p + 4, :] = re
        tmp_ref[8 + 4 * p : 12 + 4 * p, :] = im
    for t in range(2):
        speed = jnp.where(h == t, vel_ref[0], vel_ref[1])
        rot = rotation(speed, angular)
        weight = weight_of(speed, angular)
        outs = []
        for p in range(2):
            o = 136 * p + 64 * t
            re, im = corrected(g_ref, o, o + 32, 32, rot)
            fld_ref[2 * p, 8:40, :] = re
            fld_ref[2 * p + 1, 8:40, :] = im
            for c in range(2):
                r = 8 * c + 4 * p + 2 * t
                fld_ref[2 * p + c, 7:8, :] = tmp_ref[r : r + 1, :]
                fld_ref[2 * p + c, 40:41, :] = tmp_ref[r + 1 : r + 2, :]
            re, im = continued(fld_ref, p, weight, lane)
            outs.append((re, im))
            out = forward_y(re, im, fh_ref[...], fl_ref[...], twy)
            for k in range(4):
                for half in range(2):
                    d = p * 8 + 2 * k + half
                    ls = slice(128 * half, 128 * half + 128)
                    send_ref[t, d, 0:32, :] = out[k][0][:, ls]
                    send_ref[t, d, 32:64, :] = out[k][1][:, ls]
        sent(t)
        img_ref[t] = outs[0][0] * outs[1][0] - outs[0][1] * outs[1][1]


def phase_e(ready, done, recv_ref, speed, htop_ref, hbot_ref, angulars, src_ref, rcv_ref, img_ref, scr, tabs):
    fh_ref, fl_ref, twy_ref = tabs
    pc_ref, ps_ref, g_ref, fld_ref, tmp_ref, hv_ref = scr
    twy = twy_ref[...]
    pairs = []
    for i in range(4):
        o = 72 * i
        pairs += [(o, o + 32, 32), (o + 64, o + 66, 2)]

    def blocks(k, half):
        return jnp.concatenate([recv_ref[8 * i + 2 * k + half] for i in range(4)], 0)

    inverse_y(ready, blocks, pairs, fh_ref, fl_ref, twy, pc_ref, ps_ref, g_ref)
    ready(4)
    lane = lax.broadcasted_iota(jnp.int32, (32, N), 1)
    hv_ref[0:1, :] = htop_ref[2, 0:1, :]
    hv_ref[1:2, :] = hbot_ref[2, 0:1, :]
    for f in range(2):
        rot = rotation(speed, angulars[f])
        hrot = rotation(hv_ref[0:2, :], angulars[f])
        weight = weight_of(speed, angulars[f])
        outs = []
        for p in range(2):
            o = 72 * (2 * f + p)
            re, im = corrected(g_ref, o + 64, o + 66, 2, hrot)
            tmp_ref[0:2, :] = re
            tmp_ref[8:10, :] = im
            re, im = corrected(g_ref, o, o + 32, 32, rot)
            fld_ref[2 * p, 8:40, :] = re
            fld_ref[2 * p + 1, 8:40, :] = im
            for c in range(2):
                fld_ref[2 * p + c, 7:8, :] = tmp_ref[8 * c : 8 * c + 1, :]
                fld_ref[2 * p + c, 40:41, :] = tmp_ref[8 * c + 1 : 8 * c + 2, :]
            re, im = continued(fld_ref, p, weight, lane)
            outs.append((re, im))
            ref = (src_ref, rcv_ref)[p]
            ref[0, f] = re
            ref[1, f] = -im if p else im
        term = outs[0][0] * outs[1][0] - outs[0][1] * outs[1][1]
        img_ref[...] = img_ref[...] + term if f else term
        done(f)


def centered(position):
    shifted = jnp.where(position < N // 2, position, position - N)
    return shifted.astype(F32) * (2.0 * math.pi / N)


def transfer_rows(h_ref, k1, angular, yc):
    k2 = lax.broadcasted_iota(jnp.int32, (Q, 128), 0)
    lane = lax.broadcasted_iota(jnp.int32, (Q, 128), 1)
    wx = centered(4 * k2 + k1)
    wy = centered(4 * ((yc % 2) * 128 + lane) + yc // 2)
    a = angular * angular - (wx * wx + wy * wy)
    z = step_length * jnp.sqrt(jnp.abs(a))
    u = z * z
    cos = 1.0 + u * (-0.5 + u * (1.0 / 24 + u * (-1.0 / 720 + u * (1.0 / 40320))))
    sin = z * (1.0 + u * (-1.0 / 6 + u * (1.0 / 120 + u * (-1.0 / 5040))))
    travel = a >= 0.0
    scale = 1.0 / (N * N)
    h_ref[k1] = jnp.where(travel, cos, jnp.exp(-z)) * scale
    h_ref[4 + k1] = jnp.where(travel, -sin, 0.0) * scale


MESH = pl.DeviceIdType.MESH
ORDER_Z = (2, 3, 1, 0)


def mega(owner_ref, src_h, rcv_h, vel_h, fh_h, fl_h, twy_h, twx_h, oimg, so, ro, *scr):
    (src, rcv, vel, fh, fl, twy, twx, send1, recv1, send2, recv2, send3, recv3, send4, recv4,
     bh, bl, gx, ht, v1, vp, v2, pk, v4, vf, hdn, hup, htop, hbot, ibuf, ia, ip, ib, im1, i3, v3) = scr[:36]
    y_c, y_e = scr[36:42], scr[42:45] + scr[39:42]
    lsem, r1, r2, r3, r4, s1, s2, s3, s4, rv, sv, ri, si = scr[45:]
    freq, me = lax.axis_index("freq"), lax.axis_index("strip")
    x, zhi = freq // 2, freq % 2
    h, s16, zl, yc = me // 16, me % 16, me // 8, me % 8
    ang0 = omega_top * (2 * freq + 1).astype(F32) / 16
    ang1 = omega_top * (2 * freq + 2).astype(F32) / 16
    ang_h = jnp.where(h == 0, ang0, ang1)

    ins = [
        pltpu.make_async_copy(a, b, lsem.at[i])
        for i, (a, b) in enumerate(
            [(vel_h, vel), (src_h, src), (rcv_h, rcv), (fh_h, fh), (fl_h, fl), (twy_h, twy), (twx_h, twx)]
        )
    ]
    for c in ins:
        c.start()
    bar = pltpu.get_barrier_semaphore()
    for m in range(1, 32):
        pl.semaphore_signal(bar, inc=1, device_id={"freq": freq, "strip": me ^ m}, device_id_type=MESH)
    for m in range(1, 8):
        pl.semaphore_signal(bar, inc=1, device_id={"freq": freq ^ m, "strip": me}, device_id_type=MESH)
    pl.semaphore_signal(bar, inc=1, device_id={"freq": freq ^ 1, "strip": me ^ 16}, device_id_type=MESH)

    def remote(a, b, ss, rs, f, s):
        return pltpu.make_async_remote_copy(
            src_ref=a, dst_ref=b, send_sem=ss, recv_sem=rs,
            device_id={"freq": f, "strip": s}, device_id_type=MESH,
        )

    small = []

    def small_send(a, b, ss, rs, f, s):
        c = remote(a, b, ss, rs, f, s)
        c.start()
        small.append(c)

    def arrived(b, rs):
        remote(b, b, rs, rs, freq, me).wait_recv()

    def xpeer(k):
        return lax.rem(x + k, 4)

    def send_1(m):
        combo = zl ^ m
        for j in range(8):
            d = combo * 8 + (yc ^ j)
            if m == 0 and j == 0:
                pltpu.make_async_copy(send1.at[d], recv1.at[me], r1.at[me]).start()
            else:
                remote(send1.at[d], recv1.at[me], s1, r1.at[me], freq, d).start()

    for c in ins[:6]:
        c.wait()
    tw = twy[...]
    phase_a(src, rcv, send1, zl ^ 2, fh, fl, tw)
    phase_a(src, rcv, send1, zl ^ 3, fh, fl, tw)
    pl.semaphore_wait(bar, 39)

    for k in range(1, 4):
        small_send(
            vel.at[0, pl.ds(pl.multiple_of(8 * xpeer(k), 8), 8), :], v1.at[k - 1],
            sv.at[k - 1], rv.at[k - 1], 2 * xpeer(k) + zhi, me,
        )
    send_1(2)
    send_1(3)
    phase_a(src, rcv, send1, zl ^ 1, fh, fl, tw)
    send_1(1)
    phase_a(src, rcv, send1, zl, fh, fl, tw)
    send_1(0)

    for k in range(1, 4):
        arrived(v1.at[k - 1], rv.at[k - 1])
    for d in range(DEPTHS):
        acc = 0.0
        for k in range(4):
            take = jnp.where(owner_ref[d] == lax.rem(freq + 8 - 2 * k, 8), 1.0, 0.0)
            rows = v1[k - 1] if k else vel[0, pl.ds(pl.multiple_of(8 * x, 8), 8), :]
            acc = acc + take * rows
        vp[d] = acc
    for k in range(4):
        transfer_rows(ht, k, ang_h, yc)
    ins[6].wait()

    def ready1(s8):
        for n1 in range(4):
            arrived(recv1.at[8 * n1 + s8], r1.at[8 * n1 + s8])
        if s8 == 7:
            small_send(vp.at[0], v2.at[0], sv.at[3], rv.at[3], freq ^ 1, me)
            small_send(vp.at[0], v3.at[0], sv.at[4], rv.at[4], freq, me ^ 16)
            small_send(vp.at[0], v3.at[1], sv.at[12], rv.at[12], freq ^ 1, me ^ 16)

    phase_b(
        ready1,
        lambda n1, s8: (recv1[8 * n1 + s8, 0:32, :], recv1[8 * n1 + s8, 32:64, :]),
        store_16(send2), ht, fh, fl, twx, bh, bl, gx,
    )

    def send_2(m):
        d = s16 ^ m
        if m == 0:
            pltpu.make_async_copy(send2.at[d], recv2.at[s16], r2.at[s16]).start()
        else:
            remote(send2.at[d], recv2.at[s16], s2, r2.at[s16], freq, 16 * h + d).start()

    for m in range(8, 16):
        send_2(m)
    arrived(v2.at[0], rv.at[3])
    arrived(v3.at[0], rv.at[4])
    arrived(v3.at[1], rv.at[12])
    pk[0] = vp[0] + v2[0]
    pk[1] = v3[0] + v3[1]
    two = pl.ds(0, 2)
    for k in range(1, 4):
        small_send(pk.at[two], v4.at[k - 1, two], sv.at[4 + k], rv.at[4 + k], 2 * xpeer(k) + zhi, me)
    vf[0:2, pl.ds(pl.multiple_of(8 * x, 8), 8), :] = pk[0:2]
    for k in range(1, 4):
        arrived(v4.at[k - 1, two], rv.at[4 + k])
        vf[0:2, pl.ds(pl.multiple_of(8 * xpeer(4 - k), 8), 8), :] = v4[k - 1, 0:2]
    hdn[...] = jnp.zeros_like(hdn)
    hup[...] = jnp.zeros_like(hup)
    hdn[0, 0:1, :] = vf[0, 31:32, :]
    hup[0, 0:1, :] = vf[0, 0:1, :]
    below, above = lax.rem(me + 1, 32), lax.rem(me + 31, 32)
    small_send(hdn.at[0], htop.at[0], sv.at[8], rv.at[8], freq, below)
    small_send(hdn.at[0], htop.at[1], sv.at[9], rv.at[9], freq, below ^ 16)
    small_send(hup.at[0], hbot.at[0], sv.at[10], rv.at[10], freq, above)
    small_send(hup.at[0], hbot.at[1], sv.at[11], rv.at[11], freq, above ^ 16)
    for m in range(8):
        send_2(m)

    def ready2(k):
        if k == 4:
            for i, b in enumerate((htop.at[0], htop.at[1], hbot.at[0], hbot.at[1])):
                arrived(b, rv.at[8 + i])
            return
        for p in range(2):
            for half in range(2):
                i = 8 * p + 2 * k + half
                arrived(recv2.at[i], r2.at[i])
        if k == 3:
            small_send(vp.at[1], v2.at[1], sv.at[13], rv.at[13], freq ^ 1, me)

    def sent3(t):
        for m in range(16):
            d = s16 ^ m
            if m == 0:
                pltpu.make_async_copy(send3.at[t, d], recv3.at[t, s16], r3.at[t, s16]).start()
            else:
                remote(send3.at[t, d], recv3.at[t, s16], s3.at[t], r3.at[t, s16], freq, 16 * h + d).start()

    phase_c(ready2, sent3, recv2, vf, htop, hbot, h, ang_h, send3, ibuf, y_c, (fh, fl, twy))
    for k in range(1, 4):
        small_send(
            ibuf.at[:, :, pl.ds(pl.multiple_of(256 * xpeer(k), 256), 256)], ia.at[k - 1],
            si.at[k - 1], ri.at[k - 1], 2 * xpeer(k) + zhi, me,
        )

    arrived(v2.at[1], rv.at[13])
    pk[2] = vp[1] + v2[1]
    for k in range(1, 4):
        small_send(pk.at[2], v4.at[k - 1, 2], sv.at[13 + k], rv.at[13 + k], 2 * xpeer(k) + zhi, me)

    def ready3(s8):
        for t in range(2):
            for i in (s8, 8 + s8):
                arrived(recv3.at[t, i], r3.at[t, i])

    def load3(n1, s8):
        t, i = n1 // 2, 8 * (n1 % 2) + s8
        return recv3[t, i, 0:32, :], recv3[t, i, 32:64, :]

    phase_b(ready3, load3, store_32(send4), ht, fh, fl, twx, bh, bl, gx)
    vf[2, pl.ds(pl.multiple_of(8 * x, 8), 8), :] = pk[2]
    for k in range(1, 4):
        arrived(v4.at[k - 1, 2], rv.at[13 + k])
        vf[2, pl.ds(pl.multiple_of(8 * xpeer(4 - k), 8), 8), :] = v4[k - 1, 2]
    hdn[1, 0:1, :] = vf[2, 31:32, :]
    hup[1, 0:1, :] = vf[2, 0:1, :]
    small_send(hdn.at[1], htop.at[2], sv.at[17], rv.at[17], freq, below)
    small_send(hup.at[1], hbot.at[2], sv.at[18], rv.at[18], freq, above)
    for m in ORDER_Z:
        for j in range(8):
            d = me ^ (8 * m + j)
            if m == 0 and j == 0:
                pltpu.make_async_copy(send4.at[d, pl.ds(0, 68)], recv4.at[me, pl.ds(0, 68)], r4.at[me]).start()
            else:
                remote(send4.at[d, pl.ds(0, 68)], recv4.at[me, pl.ds(0, 68)], s4, r4.at[me], freq, d).start()

    for k in range(1, 4):
        arrived(ia.at[k - 1], ri.at[k - 1])
    for t in range(2):
        acc = ibuf[t, :, pl.ds(pl.multiple_of(256 * x, 256), 256)]
        for k in range(3):
            acc = acc + ia[k, t]
        ip[t, 0] = acc[:, 0:128]
        ip[t, 1] = acc[:, 128:256]
    for i, (a, b) in enumerate(((0, 1), (1, 0), (1, 1))):
        small_send(
            ip.at[h ^ b, zhi ^ a], ib.at[i], si.at[3 + i], ri.at[3 + i], freq ^ a, me ^ (16 * b)
        )

    def ready4(k):
        if k == 4:
            arrived(htop.at[2], rv.at[17])
            arrived(hbot.at[2], rv.at[18])
            return
        for i in range(4):
            for half in range(2):
                j = 8 * i + 2 * k + half
                arrived(recv4.at[j, pl.ds(0, 68)], r4.at[j])

    phase_e(ready4, lambda f: None, recv4, vf[2], htop, hbot, (ang0, ang1), so, ro, im1, y_e, (fh, fl, twy))

    for k in range(1, 8):
        small_send(
            im1.at[:, pl.ds(pl.multiple_of(128 * (freq ^ k), 128), 128)], i3.at[k - 1],
            si.at[5 + k], ri.at[5 + k], freq ^ k, me,
        )
    for i in range(3):
        arrived(ib.at[i], ri.at[3 + i])
    oimg[0] = ip[h, zhi] + ib[0] + ib[1] + ib[2]
    remote(send1.at[pl.ds(0, 31)], send1.at[pl.ds(0, 31)], s1, s1, freq, me).wait_send()
    remote(send2.at[pl.ds(0, 15)], send2.at[pl.ds(0, 15)], s2, s2, freq, me).wait_send()
    for t in range(2):
        remote(send3.at[t, pl.ds(0, 15)], send3.at[t, pl.ds(0, 15)], s3.at[t], s3.at[t], freq, me).wait_send()
    remote(send4.at[pl.ds(0, 31), pl.ds(0, 68)], send4.at[pl.ds(0, 31), pl.ds(0, 68)], s4, s4, freq, me).wait_send()
    acc = im1[:, pl.ds(pl.multiple_of(128 * freq, 128), 128)]
    for k in range(1, 8):
        arrived(i3.at[k - 1], ri.at[5 + k])
        acc = acc + i3[k - 1]
    oimg[1] = acc
    for c in small:
        c.wait_send()


def vm(*shape, dtype=F32):
    return pltpu.VMEM(shape, dtype)


def dma(*shape):
    return pltpu.SemaphoreType.DMA(shape)


SCRATCH = [
    vm(2, 2, 32, N), vm(2, 2, 32, N), vm(1, 32, N),
    vm(2 * Q, Q, dtype=BF16), vm(2 * Q, Q, dtype=BF16), vm(8, Q), vm(6, Q, 128),
    vm(32, 64, 128), vm(32, 64, 128), vm(16, 136, 128), vm(16, 136, 128),
    vm(2, 16, 64, 128), vm(2, 16, 64, 128), vm(32, 72, 128), vm(32, 72, 128),
    vm(4, Q, Q, dtype=BF16), vm(4, Q, Q, dtype=BF16), vm(4, Q, Q), vm(8, Q, 128),
    vm(3, 8, N), vm(2, 8, N), vm(2, 8, N), vm(3, 8, N), vm(3, 3, 8, N), vm(3, 32, N),
    vm(2, 8, N), vm(2, 8, N), vm(3, 8, N), vm(3, 8, N),
    vm(2, 32, N), vm(3, 2, 32, 256), vm(2, 2, 32, 128), vm(3, 32, 128), vm(32, N), vm(7, 32, 128),
    vm(2, 8, N),
    vm(272, Q), vm(272, Q), vm(4, 272, Q), vm(4, 48, N), vm(16, N), vm(8, N),
    vm(288, Q), vm(288, Q), vm(4, 288, Q),
    dma(7), dma(32), dma(16), dma(2, 16), dma(32), dma(), dma(), dma(2), dma(),
    dma(19), dma(19), dma(13), dma(13),
]


def put_out(img_i, so_i, ro_i, img_o, so_o, ro_o, img_v, so_v, ro_v, sem_in, sem_out):
    jobs = [(img_i, img_v, img_o)]
    for f in range(4):
        i = (f // 2, f % 2)
        jobs += [(so_i.at[i], so_v.at[i], so_o.at[i]), (ro_i.at[i], ro_v.at[i], ro_o.at[i])]
    loads = [pltpu.make_async_copy(a, b, sem_in.at[n]) for n, (a, b, _) in enumerate(jobs)]
    stores = [pltpu.make_async_copy(b, c, sem_out.at[n]) for n, (_, b, c) in enumerate(jobs)]
    for c in loads:
        c.start()
    for a, b in zip(loads, stores):
        a.wait()
        b.start()
    for c in stores:
        c.wait()


def finish(img, so, ro):
    any_ = pl.BlockSpec(memory_space=pl.ANY)
    return pl.pallas_call(
        put_out,
        out_shape=[jax.ShapeDtypeStruct(a.shape, F32) for a in (img, so, ro)],
        in_specs=[any_] * 3,
        out_specs=[any_] * 3,
        scratch_shapes=[vm(*a.shape) for a in (img, so, ro)] + [dma(9), dma(9)],
        name="put_out",
    )(img, so, ro)


def local(source_field, receiver_field, velocity, slice_owner):
    hi, lo, twy_np = host_tables()
    fh, fl, twy = jnp.asarray(hi), jnp.asarray(lo), jnp.asarray(twy_np)
    twx = jnp.asarray(
        np.ascontiguousarray(
            np.broadcast_to(np.concatenate([twy_np[1:4], twy_np[5:8]], 0)[:, :, None], (6, Q, 128))
        )
    )
    any_ = pl.BlockSpec(memory_space=pl.ANY)
    img, so, ro = pl.pallas_call(
        mega,
        out_shape=[
            jax.ShapeDtypeStruct((2, 32, 128), F32),
            jax.ShapeDtypeStruct((2, 2, 32, N), F32),
            jax.ShapeDtypeStruct((2, 2, 32, N), F32),
        ],
        in_specs=[pl.BlockSpec(memory_space=pltpu.SMEM)] + [any_] * 7,
        out_specs=[pl.BlockSpec(memory_space=pltpu.VMEM)] * 3,
        scratch_shapes=SCRATCH,
        compiler_params=pltpu.CompilerParams(
            collective_id=0, has_side_effects=True, vmem_limit_bytes=62 << 20
        ),
        name="continuation",
    )(slice_owner, source_field, receiver_field, velocity, fh, fl, twy, twx)
    return finish(img, so, ro)


def solution(mesh):
    return jax.shard_map(
        local,
        mesh=mesh,
        in_specs=(
            P(None, "freq", "strip", None),
            P(None, "freq", "strip", None),
            P("freq", "strip", None),
            P(),
        ),
        out_specs=(
            P(None, "strip", "freq"),
            P(None, "freq", "strip", None),
            P(None, "freq", "strip", None),
        ),
        check_vma=False,
    )
```

```python
import functools
import math

import jax
import jax.numpy as jnp
import numpy as np
from jax import lax
from jax.experimental import pallas as pl
from jax.experimental.pallas import tpu as pltpu
from jax.sharding import PartitionSpec as P

DEPTHS = 2
N = 1024
Q = 256
step_length = 0.15
omega_top = 1.2
stencil_gain = 0.05
stencil_damping = 0.1
F32 = jnp.float32
BF16 = jnp.bfloat16


def host_tables():
    i = np.arange(Q)
    ang = 2.0 * np.pi * ((i[:, None] * i[None, :]) % Q) / Q
    cs = np.concatenate([np.cos(ang), np.sin(ang)], 0).astype(np.float32)
    hi = cs.astype(jnp.bfloat16)
    lo = (cs - hi.astype(np.float32)).astype(jnp.bfloat16)
    k = np.arange(4)
    tang = 2.0 * np.pi * (k[:, None] * i[None, :]) / N
    twy = np.concatenate([np.cos(tang), np.sin(tang)], 0).astype(np.float32)
    return hi, lo, twy


def split(x):
    hi = x.astype(BF16)
    lo = (x - hi.astype(F32)).astype(BF16)
    return hi, lo


def mm(a, b):
    return jnp.dot(a, b, preferred_element_type=F32)


def radix4(x, sign):
    (ar, ai), (br, bi), (cr, ci), (dr, di) = x
    t0r, t0i, t1r, t1i = ar + cr, ai + ci, ar - cr, ai - ci
    t2r, t2i, t3r, t3i = br + dr, bi + di, br - dr, bi - di
    o0 = (t0r + t2r, t0i + t2i)
    o2 = (t0r - t2r, t0i - t2i)
    minus = (t1r + t3i, t1i - t3r)
    plus = (t1r - t3i, t1i + t3r)
    return (o0, minus, o2, plus) if sign < 0 else (o0, plus, o2, minus)


def forward_y(xr, xi, fh, fl, twy):
    rows = xr.shape[0]
    parts = [(xr[:, Q * n : Q * n + Q], xi[:, Q * n : Q * n + Q]) for n in range(4)]
    b = radix4(parts, -1)
    stack = []
    for k in range(4):
        r, m = b[k]
        if k:
            c, s = twy[k : k + 1, :], twy[4 + k : 5 + k, :]
            r, m = r * c + m * s, m * c - r * s
        stack += [r, m]
    hi, lo = split(jnp.concatenate(stack, 0))
    pc = mm(hi, fh[:Q]) + mm(lo, fh[:Q]) + mm(hi, fl[:Q])
    ps = mm(hi, fh[Q:]) + mm(lo, fh[Q:]) + mm(hi, fl[Q:])
    out = []
    for k in range(4):
        a, z, e = 2 * k * rows, (2 * k + 1) * rows, (2 * k + 2) * rows
        out.append((pc[a:z] + ps[z:e], pc[z:e] - ps[a:z]))
    return out


def phase_a(src_ref, rcv_ref, send_ref, combo, fh_ref, fl_ref, twy):
    f, p = combo // 2, combo % 2
    first = p == 0
    xr = jnp.where(first, src_ref[0, f], rcv_ref[0, f])
    xi = jnp.where(first, src_ref[1, f], -rcv_ref[1, f])
    out = forward_y(xr, xi, fh_ref[...], fl_ref[...], twy)
    for k in range(4):
        for half in range(2):
            d = combo * 8 + 2 * k + half
            send_ref[d, 0:32, :] = out[k][0][:, 128 * half : 128 * half + 128]
            send_ref[d, 32:64, :] = out[k][1][:, 128 * half : 128 * half + 128]


def phase_b(ready, load, store, h_ref, fh_ref, fl_ref, twx_ref, bh_ref, bl_ref, g_ref):
    for s8 in range(8):
        ready(s8)
        x = radix4([load(n1, s8) for n1 in range(4)], -1)
        sl = slice(32 * s8, 32 * s8 + 32)
        for k in range(4):
            r, m = x[k]
            if k:
                c, s = twx_ref[k - 1, sl, :], twx_ref[2 + k, sl, :]
                r, m = r * c + m * s, m * c - r * s
            rh, rl = split(r)
            mh, ml = split(m)
            bh_ref[k, sl, 0:128] = rh
            bl_ref[k, sl, 0:128] = rl
            bh_ref[k, sl, 128:256] = mh
            bl_ref[k, sl, 128:256] = ml
    for k in range(4):
        fh, fl = fh_ref[...], fl_ref[...]
        bh = bh_ref[k]
        pr = mm(fh, bh) + mm(fl, bh) + mm(fh, bl_ref[k])
        re = pr[:Q, :128] + pr[Q:, 128:]
        im = pr[:Q, 128:] - pr[Q:, :128]
        hr, hi_ = h_ref[k], h_ref[4 + k]
        zr = re * hr - im * hi_
        zi = re * hi_ + im * hr
        zh, zl = split(jnp.concatenate([zr, zi], 1))
        pr = mm(fh, zh) + mm(fl, zh) + mm(fh, zl)
        re = pr[:Q, :128] - pr[Q:, 128:]
        im = pr[:Q, 128:] + pr[Q:, :128]
        if k:
            c, s = twx_ref[k - 1], twx_ref[2 + k]
            re, im = re * c - im * s, im * c + re * s
        g_ref[k, :, 0:128] = re
        g_ref[k, :, 128:256] = im
    for s8 in range(8):
        sl = slice(32 * s8, 32 * s8 + 32)
        x = radix4([(g_ref[k, sl, 0:128], g_ref[k, sl, 128:256]) for k in range(4)], 1)
        for n1 in range(4):
            store(8 * n1 + s8, *x[n1])


def store_16(send_ref):
    zero = jnp.zeros((1, 128), F32)

    def store(s, re, im):
        d, t = s % 16, s // 16
        send_ref[d, 64 * t : 64 * t + 32, :] = re
        send_ref[d, 64 * t + 32 : 64 * t + 64, :] = im
        if s < 31:
            d, t = (s + 1) % 16, (s + 1) // 16
            send_ref[d, 128 + 2 * t : 129 + 2 * t, :] = re[31:32]
            send_ref[d, 132 + 2 * t : 133 + 2 * t, :] = im[31:32]
        else:
            send_ref[15, 131:132, :] = zero
            send_ref[15, 135:136, :] = zero
        if s > 0:
            d, t = (s - 1) % 16, (s - 1) // 16
            send_ref[d, 129 + 2 * t : 130 + 2 * t, :] = re[0:1]
            send_ref[d, 133 + 2 * t : 134 + 2 * t, :] = im[0:1]
        else:
            send_ref[0, 128:129, :] = zero
            send_ref[0, 132:133, :] = zero

    return store


def store_32(send_ref):
    zero = jnp.zeros((1, 128), F32)

    def store(s, re, im):
        send_ref[s, 0:32, :] = re
        send_ref[s, 32:64, :] = im
        if s < 31:
            send_ref[s + 1, 64:65, :] = re[31:32]
            send_ref[s + 1, 66:67, :] = im[31:32]
        else:
            send_ref[31, 65:66, :] = zero
            send_ref[31, 67:68, :] = zero
        send_ref[s, 68:72, :] = jnp.zeros((4, 128), F32)
        if s > 0:
            send_ref[s - 1, 65:66, :] = re[0:1]
            send_ref[s - 1, 67:68, :] = im[0:1]
        else:
            send_ref[0, 64:65, :] = zero
            send_ref[0, 66:67, :] = zero

    return store


def inverse_y(ready, blocks, pairs, fh_ref, fl_ref, twy, pc_ref, ps_ref, g_ref):
    for k in range(4):
        ready(k)
        x = jnp.concatenate([blocks(k, 0), blocks(k, 1)], 1)
        hi, lo = split(x)
        pc_ref[...] = mm(hi, fh_ref[:Q]) + mm(lo, fh_ref[:Q]) + mm(hi, fl_ref[:Q])
        ps_ref[...] = mm(hi, fh_ref[Q:]) + mm(lo, fh_ref[Q:]) + mm(hi, fl_ref[Q:])
        for a, b, n in pairs:
            re = pc_ref[a : a + n] - ps_ref[b : b + n]
            im = pc_ref[b : b + n] + ps_ref[a : a + n]
            if k:
                c, s = twy[k : k + 1, :], twy[4 + k : 5 + k, :]
                re, im = re * c - im * s, im * c + re * s
            g_ref[k, a : a + n, :] = re
            g_ref[k, b : b + n, :] = im


def corrected(g_ref, a, b, n, rot):
    x = radix4([(g_ref[k, a : a + n, :], g_ref[k, b : b + n, :]) for k in range(4)], 1)
    re = jnp.concatenate([x[i][0] for i in range(4)], 1)
    im = jnp.concatenate([x[i][1] for i in range(4)], 1)
    c, s = rot
    return re * c + im * s, im * c - re * s


def rotation(speed, angular):
    ph = angular * step_length * (1.0 / speed - 1.0)
    u = ph * ph
    c = 1.0 + u * (-0.5 + u * (1.0 / 24 + u * (-1.0 / 720)))
    s = ph * (1.0 + u * (-1.0 / 6 + u * (1.0 / 120 + u * (-1.0 / 5040))))
    return c, s


def laplace(ref, idx, lane):
    mid = ref[idx, 8:40, :]
    left = jnp.where(lane == 0, 0.0, pltpu.roll(mid, 1, 1))
    right = jnp.where(lane == N - 1, 0.0, pltpu.roll(mid, N - 1, 1))
    beside = ref[idx, 9:41, :] + ref[idx, 7:39, :]
    return mid, beside + left + right - 4.0 * mid


def continued(fld_ref, i, weight, lane):
    pr, lr = laplace(fld_ref, 2 * i, lane)
    pi_, li = laplace(fld_ref, 2 * i + 1, lane)
    return (
        pr + weight * (stencil_damping * lr + li),
        pi_ + weight * (stencil_damping * li - lr),
    )


def weight_of(speed, angular):
    return stencil_gain * (speed * speed - 1.0) * angular / omega_top


def phase_c(ready, sent, recv_ref, vel_ref, htop_ref, hbot_ref, h, angular, send_ref, img_ref, scr, tabs):
    fh_ref, fl_ref, twy_ref = tabs
    pc_ref, ps_ref, g_ref, fld_ref, tmp_ref, hv_ref = scr
    twy = twy_ref[...]
    pairs = []
    for p in range(2):
        o = 136 * p
        pairs += [(o, o + 32, 32), (o + 64, o + 96, 32), (o + 128, o + 132, 4)]

    def blocks(k, half):
        return jnp.concatenate([recv_ref[2 * k + half], recv_ref[8 + 2 * k + half]], 0)

    inverse_y(ready, blocks, pairs, fh_ref, fl_ref, twy, pc_ref, ps_ref, g_ref)
    ready(4)
    lane = lax.broadcasted_iota(jnp.int32, (32, N), 1)
    for t in range(2):
        own = h == t
        hv_ref[2 * t : 2 * t + 1, :] = jnp.where(own, htop_ref[0, 0:1, :], htop_ref[1, 0:1, :])
        hv_ref[2 * t + 1 : 2 * t + 2, :] = jnp.where(own, hbot_ref[0, 0:1, :], hbot_ref[1, 0:1, :])
    hrot = rotation(hv_ref[0:4, :], angular)
    for p in range(2):
        o = 136 * p + 128
        re, im = corrected(g_ref, o, o + 4, 4, hrot)
        tmp_ref[4 * p : 4 * p + 4, :] = re
        tmp_ref[8 + 4 * p : 12 + 4 * p, :] = im
    for t in range(2):
        speed = jnp.where(h == t, vel_ref[0], vel_ref[1])
        rot = rotation(speed, angular)
        weight = weight_of(speed, angular)
        outs = []
        for p in range(2):
            o = 136 * p + 64 * t
            re, im = corrected(g_ref, o, o + 32, 32, rot)
            fld_ref[2 * p, 8:40, :] = re
            fld_ref[2 * p + 1, 8:40, :] = im
            for c in range(2):
                r = 8 * c + 4 * p + 2 * t
                fld_ref[2 * p + c, 7:8, :] = tmp_ref[r : r + 1, :]
                fld_ref[2 * p + c, 40:41, :] = tmp_ref[r + 1 : r + 2, :]
            re, im = continued(fld_ref, p, weight, lane)
            outs.append((re, im))
            out = forward_y(re, im, fh_ref[...], fl_ref[...], twy)
            for k in range(4):
                for half in range(2):
                    d = p * 8 + 2 * k + half
                    ls = slice(128 * half, 128 * half + 128)
                    send_ref[t, d, 0:32, :] = out[k][0][:, ls]
                    send_ref[t, d, 32:64, :] = out[k][1][:, ls]
        sent(t)
        img_ref[t] = outs[0][0] * outs[1][0] - outs[0][1] * outs[1][1]


def phase_e(ready, done, recv_ref, speed, htop_ref, hbot_ref, angulars, src_ref, rcv_ref, img_ref, scr, tabs):
    fh_ref, fl_ref, twy_ref = tabs
    pc_ref, ps_ref, g_ref, fld_ref, tmp_ref, hv_ref = scr
    twy = twy_ref[...]
    pairs = []
    for i in range(4):
        o = 72 * i
        pairs += [(o, o + 32, 32), (o + 64, o + 66, 2)]

    def blocks(k, half):
        return jnp.concatenate([recv_ref[8 * i + 2 * k + half] for i in range(4)], 0)

    inverse_y(ready, blocks, pairs, fh_ref, fl_ref, twy, pc_ref, ps_ref, g_ref)
    ready(4)
    lane = lax.broadcasted_iota(jnp.int32, (32, N), 1)
    hv_ref[0:1, :] = htop_ref[2, 0:1, :]
    hv_ref[1:2, :] = hbot_ref[2, 0:1, :]
    for f in range(2):
        rot = rotation(speed, angulars[f])
        hrot = rotation(hv_ref[0:2, :], angulars[f])
        weight = weight_of(speed, angulars[f])
        outs = []
        for p in range(2):
            o = 72 * (2 * f + p)
            re, im = corrected(g_ref, o + 64, o + 66, 2, hrot)
            tmp_ref[0:2, :] = re
            tmp_ref[8:10, :] = im
            re, im = corrected(g_ref, o, o + 32, 32, rot)
            fld_ref[2 * p, 8:40, :] = re
            fld_ref[2 * p + 1, 8:40, :] = im
            for c in range(2):
                fld_ref[2 * p + c, 7:8, :] = tmp_ref[8 * c : 8 * c + 1, :]
                fld_ref[2 * p + c, 40:41, :] = tmp_ref[8 * c + 1 : 8 * c + 2, :]
            re, im = continued(fld_ref, p, weight, lane)
            outs.append((re, im))
            ref = (src_ref, rcv_ref)[p]
            ref[0, f] = re
            ref[1, f] = -im if p else im
        term = outs[0][0] * outs[1][0] - outs[0][1] * outs[1][1]
        img_ref[...] = img_ref[...] + term if f else term
        done(f)


def centered(position):
    shifted = jnp.where(position < N // 2, position, position - N)
    return shifted.astype(F32) * (2.0 * math.pi / N)


def transfer_rows(h_ref, k1, angular, yc):
    k2 = lax.broadcasted_iota(jnp.int32, (Q, 128), 0)
    lane = lax.broadcasted_iota(jnp.int32, (Q, 128), 1)
    wx = centered(4 * k2 + k1)
    wy = centered(4 * ((yc % 2) * 128 + lane) + yc // 2)
    a = angular * angular - (wx * wx + wy * wy)
    z = step_length * jnp.sqrt(jnp.abs(a))
    u = z * z
    cos = 1.0 + u * (-0.5 + u * (1.0 / 24 + u * (-1.0 / 720 + u * (1.0 / 40320))))
    sin = z * (1.0 + u * (-1.0 / 6 + u * (1.0 / 120 + u * (-1.0 / 5040))))
    travel = a >= 0.0
    scale = 1.0 / (N * N)
    h_ref[k1] = jnp.where(travel, cos, jnp.exp(-z)) * scale
    h_ref[4 + k1] = jnp.where(travel, -sin, 0.0) * scale


MESH = pl.DeviceIdType.MESH
ORDER_Z = (2, 3, 1, 0)


def mega(owner_ref, src_h, rcv_h, vel_h, fh_h, fl_h, twy_h, twx_h, oimg, so, ro, *scr):
    (src, rcv, vel, fh, fl, twy, twx, send1, recv1, send2, recv2, send3, recv3, send4, recv4,
     bh, bl, gx, ht, v1, vp, v2, pk, v4, vf, hdn, hup, htop, hbot, ibuf, ia, ip, ib, im1, i3, v3) = scr[:36]
    y_c, y_e = scr[36:42], scr[42:45] + scr[39:42]
    lsem, r1, r2, r3, r4, s1, s2, s3, s4, rv, sv, ri, si = scr[45:]
    freq, me = lax.axis_index("freq"), lax.axis_index("strip")
    x, zhi = freq // 2, freq % 2
    h, s16, zl, yc = me // 16, me % 16, me // 8, me % 8
    ang0 = omega_top * (2 * freq + 1).astype(F32) / 16
    ang1 = omega_top * (2 * freq + 2).astype(F32) / 16
    ang_h = jnp.where(h == 0, ang0, ang1)

    ins = [
        pltpu.make_async_copy(a, b, lsem.at[i])
        for i, (a, b) in enumerate(
            [(vel_h, vel), (src_h, src), (rcv_h, rcv), (fh_h, fh), (fl_h, fl), (twy_h, twy), (twx_h, twx)]
        )
    ]
    for c in ins:
        c.start()
    bar = pltpu.get_barrier_semaphore()
    for m in range(1, 32):
        pl.semaphore_signal(bar, inc=1, device_id={"freq": freq, "strip": me ^ m}, device_id_type=MESH)
    for m in range(1, 8):
        pl.semaphore_signal(bar, inc=1, device_id={"freq": freq ^ m, "strip": me}, device_id_type=MESH)
    pl.semaphore_signal(bar, inc=1, device_id={"freq": freq ^ 1, "strip": me ^ 16}, device_id_type=MESH)

    def remote(a, b, ss, rs, f, s):
        return pltpu.make_async_remote_copy(
            src_ref=a, dst_ref=b, send_sem=ss, recv_sem=rs,
            device_id={"freq": f, "strip": s}, device_id_type=MESH,
        )

    small = []

    def small_send(a, b, ss, rs, f, s):
        c = remote(a, b, ss, rs, f, s)
        c.start()
        small.append(c)

    def arrived(b, rs):
        remote(b, b, rs, rs, freq, me).wait_recv()

    def xpeer(k):
        return lax.rem(x + k, 4)

    def send_1(m):
        combo = zl ^ m
        for j in range(8):
            d = combo * 8 + (yc ^ j)
            if m == 0 and j == 0:
                pltpu.make_async_copy(send1.at[d], recv1.at[me], r1.at[me]).start()
            else:
                remote(send1.at[d], recv1.at[me], s1, r1.at[me], freq, d).start()

    for c in ins[:6]:
        c.wait()
    tw = twy[...]
    phase_a(src, rcv, send1, zl ^ 2, fh, fl, tw)
    phase_a(src, rcv, send1, zl ^ 3, fh, fl, tw)
    pl.semaphore_wait(bar, 39)

    for k in range(1, 4):
        small_send(
            vel.at[0, pl.ds(pl.multiple_of(8 * xpeer(k), 8), 8), :], v1.at[k - 1],
            sv.at[k - 1], rv.at[k - 1], 2 * xpeer(k) + zhi, me,
        )
    send_1(2)
    send_1(3)
    phase_a(src, rcv, send1, zl ^ 1, fh, fl, tw)
    send_1(1)
    phase_a(src, rcv, send1, zl, fh, fl, tw)
    send_1(0)

    for k in range(1, 4):
        arrived(v1.at[k - 1], rv.at[k - 1])
    for d in range(DEPTHS):
        acc = 0.0
        for k in range(4):
            take = jnp.where(owner_ref[d] == lax.rem(freq + 8 - 2 * k, 8), 1.0, 0.0)
            rows = v1[k - 1] if k else vel[0, pl.ds(pl.multiple_of(8 * x, 8), 8), :]
            acc = acc + take * rows
        vp[d] = acc
    for k in range(4):
        transfer_rows(ht, k, ang_h, yc)
    ins[6].wait()

    def ready1(s8):
        for n1 in range(4):
            arrived(recv1.at[8 * n1 + s8], r1.at[8 * n1 + s8])
        if s8 == 7:
            small_send(vp.at[0], v2.at[0], sv.at[3], rv.at[3], freq ^ 1, me)
            small_send(vp.at[0], v3.at[0], sv.at[4], rv.at[4], freq, me ^ 16)
            small_send(vp.at[0], v3.at[1], sv.at[12], rv.at[12], freq ^ 1, me ^ 16)

    phase_b(
        ready1,
        lambda n1, s8: (recv1[8 * n1 + s8, 0:32, :], recv1[8 * n1 + s8, 32:64, :]),
        store_16(send2), ht, fh, fl, twx, bh, bl, gx,
    )

    def send_2(m):
        d = s16 ^ m
        if m == 0:
            pltpu.make_async_copy(send2.at[d], recv2.at[s16], r2.at[s16]).start()
        else:
            remote(send2.at[d], recv2.at[s16], s2, r2.at[s16], freq, 16 * h + d).start()

    for m in range(8, 16):
        send_2(m)
    arrived(v2.at[0], rv.at[3])
    arrived(v3.at[0], rv.at[4])
    arrived(v3.at[1], rv.at[12])
    pk[0] = vp[0] + v2[0]
    pk[1] = v3[0] + v3[1]
    two = pl.ds(0, 2)
    for k in range(1, 4):
        small_send(pk.at[two], v4.at[k - 1, two], sv.at[4 + k], rv.at[4 + k], 2 * xpeer(k) + zhi, me)
    vf[0:2, pl.ds(pl.multiple_of(8 * x, 8), 8), :] = pk[0:2]
    for k in range(1, 4):
        arrived(v4.at[k - 1, two], rv.at[4 + k])
        vf[0:2, pl.ds(pl.multiple_of(8 * xpeer(4 - k), 8), 8), :] = v4[k - 1, 0:2]
    hdn[...] = jnp.zeros_like(hdn)
    hup[...] = jnp.zeros_like(hup)
    hdn[0, 0:1, :] = vf[0, 31:32, :]
    hup[0, 0:1, :] = vf[0, 0:1, :]
    below, above = lax.rem(me + 1, 32), lax.rem(me + 31, 32)
    small_send(hdn.at[0], htop.at[0], sv.at[8], rv.at[8], freq, below)
    small_send(hdn.at[0], htop.at[1], sv.at[9], rv.at[9], freq, below ^ 16)
    small_send(hup.at[0], hbot.at[0], sv.at[10], rv.at[10], freq, above)
    small_send(hup.at[0], hbot.at[1], sv.at[11], rv.at[11], freq, above ^ 16)
    for m in range(8):
        send_2(m)

    def ready2(k):
        if k == 4:
            for i, b in enumerate((htop.at[0], htop.at[1], hbot.at[0], hbot.at[1])):
                arrived(b, rv.at[8 + i])
            return
        for p in range(2):
            for half in range(2):
                i = 8 * p + 2 * k + half
                arrived(recv2.at[i], r2.at[i])
        if k == 3:
            small_send(vp.at[1], v2.at[1], sv.at[13], rv.at[13], freq ^ 1, me)

    def sent3(t):
        for m in (1, 8, 2, 9, 3, 10, 4, 11, 5, 12, 6, 13, 7, 14, 15, 0):
            d = s16 ^ m
            if m == 0:
                pltpu.make_async_copy(send3.at[t, d], recv3.at[t, s16], r3.at[t, s16]).start()
            else:
                remote(send3.at[t, d], recv3.at[t, s16], s3.at[t], r3.at[t, s16], freq, 16 * h + d).start()

    phase_c(ready2, sent3, recv2, vf, htop, hbot, h, ang_h, send3, ibuf, y_c, (fh, fl, twy))
    for k in range(1, 4):
        small_send(
            ibuf.at[:, :, pl.ds(pl.multiple_of(256 * xpeer(k), 256), 256)], ia.at[k - 1],
            si.at[k - 1], ri.at[k - 1], 2 * xpeer(k) + zhi, me,
        )

    arrived(v2.at[1], rv.at[13])
    pk[2] = vp[1] + v2[1]
    for k in range(1, 4):
        small_send(pk.at[2], v4.at[k - 1, 2], sv.at[13 + k], rv.at[13 + k], 2 * xpeer(k) + zhi, me)

    def ready3(s8):
        for t in range(2):
            for i in (s8, 8 + s8):
                arrived(recv3.at[t, i], r3.at[t, i])

    def load3(n1, s8):
        t, i = n1 // 2, 8 * (n1 % 2) + s8
        return recv3[t, i, 0:32, :], recv3[t, i, 32:64, :]

    phase_b(ready3, load3, store_32(send4), ht, fh, fl, twx, bh, bl, gx)
    vf[2, pl.ds(pl.multiple_of(8 * x, 8), 8), :] = pk[2]
    for k in range(1, 4):
        arrived(v4.at[k - 1, 2], rv.at[13 + k])
        vf[2, pl.ds(pl.multiple_of(8 * xpeer(4 - k), 8), 8), :] = v4[k - 1, 2]
    hdn[1, 0:1, :] = vf[2, 31:32, :]
    hup[1, 0:1, :] = vf[2, 0:1, :]
    small_send(hdn.at[1], htop.at[2], sv.at[17], rv.at[17], freq, below)
    small_send(hup.at[1], hbot.at[2], sv.at[18], rv.at[18], freq, above)
    for m in ORDER_Z:
        for j in range(8):
            d = me ^ (8 * m + j)
            if m == 0 and j == 0:
                pltpu.make_async_copy(send4.at[d, pl.ds(0, 68)], recv4.at[me, pl.ds(0, 68)], r4.at[me]).start()
            else:
                remote(send4.at[d, pl.ds(0, 68)], recv4.at[me, pl.ds(0, 68)], s4, r4.at[me], freq, d).start()

    for k in range(1, 4):
        arrived(ia.at[k - 1], ri.at[k - 1])
    for t in range(2):
        acc = ibuf[t, :, pl.ds(pl.multiple_of(256 * x, 256), 256)]
        for k in range(3):
            acc = acc + ia[k, t]
        ip[t, 0] = acc[:, 0:128]
        ip[t, 1] = acc[:, 128:256]
    for i, (a, b) in enumerate(((0, 1), (1, 0), (1, 1))):
        small_send(
            ip.at[h ^ b, zhi ^ a], ib.at[i], si.at[3 + i], ri.at[3 + i], freq ^ a, me ^ (16 * b)
        )

    def ready4(k):
        if k == 4:
            arrived(htop.at[2], rv.at[17])
            arrived(hbot.at[2], rv.at[18])
            return
        for i in range(4):
            for half in range(2):
                j = 8 * i + 2 * k + half
                arrived(recv4.at[j, pl.ds(0, 68)], r4.at[j])

    phase_e(ready4, lambda f: None, recv4, vf[2], htop, hbot, (ang0, ang1), so, ro, im1, y_e, (fh, fl, twy))

    for k in range(1, 8):
        small_send(
            im1.at[:, pl.ds(pl.multiple_of(128 * (freq ^ k), 128), 128)], i3.at[k - 1],
            si.at[5 + k], ri.at[5 + k], freq ^ k, me,
        )
    for i in range(3):
        arrived(ib.at[i], ri.at[3 + i])
    oimg[0] = ip[h, zhi] + ib[0] + ib[1] + ib[2]
    remote(send1.at[pl.ds(0, 31)], send1.at[pl.ds(0, 31)], s1, s1, freq, me).wait_send()
    remote(send2.at[pl.ds(0, 15)], send2.at[pl.ds(0, 15)], s2, s2, freq, me).wait_send()
    for t in range(2):
        remote(send3.at[t, pl.ds(0, 15)], send3.at[t, pl.ds(0, 15)], s3.at[t], s3.at[t], freq, me).wait_send()
    remote(send4.at[pl.ds(0, 31), pl.ds(0, 68)], send4.at[pl.ds(0, 31), pl.ds(0, 68)], s4, s4, freq, me).wait_send()
    acc = im1[:, pl.ds(pl.multiple_of(128 * freq, 128), 128)]
    for k in range(1, 8):
        arrived(i3.at[k - 1], ri.at[5 + k])
        acc = acc + i3[k - 1]
    oimg[1] = acc
    for c in small:
        c.wait_send()


def vm(*shape, dtype=F32):
    return pltpu.VMEM(shape, dtype)


def dma(*shape):
    return pltpu.SemaphoreType.DMA(shape)


SCRATCH = [
    vm(2, 2, 32, N), vm(2, 2, 32, N), vm(1, 32, N),
    vm(2 * Q, Q, dtype=BF16), vm(2 * Q, Q, dtype=BF16), vm(8, Q), vm(6, Q, 128),
    vm(32, 64, 128), vm(32, 64, 128), vm(16, 136, 128), vm(16, 136, 128),
    vm(2, 16, 64, 128), vm(2, 16, 64, 128), vm(32, 72, 128), vm(32, 72, 128),
    vm(4, Q, Q, dtype=BF16), vm(4, Q, Q, dtype=BF16), vm(4, Q, Q), vm(8, Q, 128),
    vm(3, 8, N), vm(2, 8, N), vm(2, 8, N), vm(3, 8, N), vm(3, 3, 8, N), vm(3, 32, N),
    vm(2, 8, N), vm(2, 8, N), vm(3, 8, N), vm(3, 8, N),
    vm(2, 32, N), vm(3, 2, 32, 256), vm(2, 2, 32, 128), vm(3, 32, 128), vm(32, N), vm(7, 32, 128),
    vm(2, 8, N),
    vm(272, Q), vm(272, Q), vm(4, 272, Q), vm(4, 48, N), vm(16, N), vm(8, N),
    vm(288, Q), vm(288, Q), vm(4, 288, Q),
    dma(7), dma(32), dma(16), dma(2, 16), dma(32), dma(), dma(), dma(2), dma(),
    dma(19), dma(19), dma(13), dma(13),
]


def put_out(img_i, so_i, ro_i, img_o, so_o, ro_o, img_v, so_v, ro_v, sem_in, sem_out):
    jobs = [(img_i, img_v, img_o)]
    for f in range(4):
        i = (f // 2, f % 2)
        jobs += [(so_i.at[i], so_v.at[i], so_o.at[i]), (ro_i.at[i], ro_v.at[i], ro_o.at[i])]
    loads = [pltpu.make_async_copy(a, b, sem_in.at[n]) for n, (a, b, _) in enumerate(jobs)]
    stores = [pltpu.make_async_copy(b, c, sem_out.at[n]) for n, (_, b, c) in enumerate(jobs)]
    for c in loads:
        c.start()
    for a, b in zip(loads, stores):
        a.wait()
        b.start()
    for c in stores:
        c.wait()


def finish(img, so, ro):
    any_ = pl.BlockSpec(memory_space=pl.ANY)
    return pl.pallas_call(
        put_out,
        out_shape=[jax.ShapeDtypeStruct(a.shape, F32) for a in (img, so, ro)],
        in_specs=[any_] * 3,
        out_specs=[any_] * 3,
        scratch_shapes=[vm(*a.shape) for a in (img, so, ro)] + [dma(9), dma(9)],
        name="put_out",
    )(img, so, ro)


def local(source_field, receiver_field, velocity, slice_owner):
    hi, lo, twy_np = host_tables()
    fh, fl, twy = jnp.asarray(hi), jnp.asarray(lo), jnp.asarray(twy_np)
    twx = jnp.asarray(
        np.ascontiguousarray(
            np.broadcast_to(np.concatenate([twy_np[1:4], twy_np[5:8]], 0)[:, :, None], (6, Q, 128))
        )
    )
    any_ = pl.BlockSpec(memory_space=pl.ANY)
    img, so, ro = pl.pallas_call(
        mega,
        out_shape=[
            jax.ShapeDtypeStruct((2, 32, 128), F32),
            jax.ShapeDtypeStruct((2, 2, 32, N), F32),
            jax.ShapeDtypeStruct((2, 2, 32, N), F32),
        ],
        in_specs=[pl.BlockSpec(memory_space=pltpu.SMEM)] + [any_] * 7,
        out_specs=[pl.BlockSpec(memory_space=pltpu.VMEM)] * 3,
        scratch_shapes=SCRATCH,
        compiler_params=pltpu.CompilerParams(
            collective_id=0, has_side_effects=True, vmem_limit_bytes=62 << 20
        ),
        name="continuation",
    )(slice_owner, source_field, receiver_field, velocity, fh, fl, twy, twx)
    return finish(img, so, ro)


def solution(mesh):
    return jax.shard_map(
        local,
        mesh=mesh,
        in_specs=(
            P(None, "freq", "strip", None),
            P(None, "freq", "strip", None),
            P("freq", "strip", None),
            P(),
        ),
        out_specs=(
            P(None, "strip", "freq"),
            P(None, "freq", "strip", None),
            P(None, "freq", "strip", None),
        ),
        check_vma=False,
    )
```
